32 devices in a mesh: grp: 4 (over y, x), shard: 8 (over z, core).
Axes of the slice: x: 2, y: 2, z: 4, core: 2. Of those that a mesh axis runs over, the one named last changes fastest.
Arguments:
- partials: bfloat16 [4, 1536, 2, 4096], P('grp', 'shard'), may hold values from -225 to 225
- weights: float32 [1536, 2, 4096], P('shard'), may hold values from -4 to 4
- subspace: bfloat16 [1536, 2, 256], P('shard'), may hold values from -6 to 6
- moment_one: float32 [4096, 2, 256], P('shard'), may hold values from -2 to 2
- moment_two: float32 [4096, 2, 256], P('shard'), may hold values from 0.001 to 0.1
Outputs:
- new_weights: float32 [1536, 2, 4096], P('shard')
- new_moment_one: float32 [4096, 2, 256], P('shard')
- new_moment_two: float32 [4096, 2, 256], P('shard')
- new_subspace: bfloat16 [1536, 2, 256], P('shard')
The draws below stay inside these ranges and needn't reach their ends.
All inputs are finite; a program needn't handle non-finite values.
Results may differ from the reference program's by a relative error of at most 0.01.
Values may be sent and summed in bfloat16 or wider, within the bound.
No kernel may reach another device: no remote copies, remote signals or barrier semaphores. Data moves between devices by JAX's collectives and lax.ppermute only.
A program may use at most 128 MiB of HBM per device.

```python
import math
import jax
import jax.numpy as jnp
from jax import lax

D = 1536
FF = 4096
RANK = 256
MATS = 2
N_GRP = 4


def draw_partials(key, part):
    key_rows, key_cols, key_own = jax.random.split(key, 3)
    row_index = jnp.arange(D, dtype=jnp.float32)
    rising = jnp.exp(math.log(3.0) * row_index / (D - 1))
    row_scale = rising * jnp.exp(jax.random.uniform(key_rows, (D,), jnp.float32, math.log(0.5), math.log(5.0)))
    col_scale = jnp.exp(jax.random.uniform(key_cols, (MATS, FF), jnp.float32, math.log(0.3), math.log(3.0)))
    base = jax.random.normal(key_own, (N_GRP, D, MATS, FF), jnp.float32)
    base = jnp.clip(base, -5.0, 5.0)
    values = base * row_scale[None, :, None, None] * col_scale[None, None, :, :]
    return values.astype(jnp.bfloat16)


def levels(stream_key, dims, cuts, low, top_value):
    def one(dim, blocks):
        steps = jax.random.uniform(jax.random.fold_in(jax.random.fold_in(stream_key, 6), dim), (blocks,), jnp.float32, low / len(cuts), top_value / len(cuts))
        return jnp.repeat(jnp.exp(steps), dims[dim] // blocks).reshape((-1,) + (1,) * (len(dims) - dim - 1))

    level = one(*cuts[0])
    for cut in cuts[1:]:
        level = level * one(*cut)
    return level


def bell_draw(own_key, dims, width, reach, cuts=(), held_as=jnp.bfloat16):
    result = width * jax.random.normal(own_key, dims, jnp.float32)
    if cuts:
        result = result * levels(own_key, dims, cuts, -0.22, 0.18)
    return jnp.clip(result, -reach, reach).astype(held_as)


def setup_inputs(seed: int = 0) -> dict:
    key_of = jax.random.split(jax.random.key(seed), 6)
    partials = draw_partials(jax.random.fold_in(key_of[5], 71), 0)
    weights = bell_draw(key_of[1], (D, MATS, FF), 0.5, 4.0, ((0, 8),), jnp.float32)
    subspace = bell_draw(key_of[2], (D, MATS, RANK), 1.0, 6.0, ((0, 8),))
    moment_one = bell_draw(key_of[3], (FF, MATS, RANK), 0.3, 2.0, ((0, 8),), jnp.float32)
    moment_two = jnp.clip(jnp.exp(math.log(0.1) - 4.6051702 * jax.random.uniform(key_of[4], (FF, MATS, RANK), jnp.float32) ** levels(key_of[4], (FF, MATS, RANK), ((0, 8),), -0.2, 0.2)), 0.001, 0.1)
    return dict(partials=partials, weights=weights, subspace=subspace, moment_one=moment_one, moment_two=moment_two)


first_fix = 1.0 - 0.9 ** 10
second_fix = 1.0 - 0.999 ** 10

def reference(partials, weights, subspace, moment_one, moment_two):
    gradient = lax.optimization_barrier(jnp.sum(partials.astype(jnp.float32), axis=0)).astype(jnp.bfloat16)
    inv_root = 1.0 / math.sqrt(D)
    projected = jnp.einsum('dmf,dmk->fmk', gradient.astype(jnp.float32), subspace.astype(jnp.float32)) * inv_root
    new_moment_one = 0.9 * moment_one + 0.1 * projected
    new_moment_two = 0.999 * moment_two + 0.001 * projected * projected
    direction = (new_moment_one / first_fix / (jnp.sqrt(new_moment_two / second_fix) + 1e-08)).astype(jnp.bfloat16)
    increment = jnp.einsum('dmk,fmk->dmf', subspace.astype(jnp.float32), direction.astype(jnp.float32))
    new_weights = weights - increment * inv_root
    projected_half = projected.astype(jnp.bfloat16)
    spanned = jnp.einsum('dmf,fmk->dmk', gradient.astype(jnp.float32), projected_half.astype(jnp.float32))
    gram_matrix = jnp.einsum('dmk,dml->mkl', spanned, spanned, precision=lax.Precision.HIGHEST)
    normalizer = 1.7 / jnp.sqrt(jnp.sqrt(lax.optimization_barrier(jnp.sum(gram_matrix * gram_matrix, axis=(1, 2)))) + 1e-06)
    oriented = spanned * normalizer[None, :, None]
    ortho_gram = gram_matrix * (normalizer * normalizer)[:, None, None]
    polished = 1.5 * oriented - 0.5 * jnp.einsum('dmk,mkl->dml', oriented, ortho_gram, precision=lax.Precision.HIGHEST)
    new_subspace = (math.sqrt(D) * polished).astype(jnp.bfloat16)
    return (new_weights, new_moment_one, new_moment_two, new_subspace)
```

```python
import math

import jax
import jax.numpy as jnp
from jax import lax
from jax.experimental import pallas as pl
from jax.experimental.pallas import tpu as pltpu
from jax.sharding import PartitionSpec as P

D = 1536
bf16 = jnp.bfloat16
f32 = jnp.float32
inv_root = 1.0 / math.sqrt(D)
first_fix = 1.0 - 0.9**10
second_fix = 1.0 - 0.999**10


def plain(partials, weights, subspace, moment_one, moment_two):
    gradient = lax.psum(partials[0], "grp")
    projected = lax.psum_scatter(
        jnp.einsum("dmf,dmk->fmk", gradient, subspace, preferred_element_type=f32) * inv_root,
        "shard",
        scatter_dimension=0,
        tiled=True,
    )
    new_one, new_two, direction = adam(projected, moment_one, moment_two)
    increment = jnp.einsum(
        "dmk,fmk->dmf",
        subspace,
        lax.all_gather(direction, "shard", axis=0, tiled=True),
        preferred_element_type=f32,
    )
    new_weights = weights - increment * inv_root
    spanned = jnp.einsum(
        "dmf,fmk->dmk",
        gradient,
        lax.all_gather(projected.astype(bf16), "shard", axis=0, tiled=True),
        preferred_element_type=f32,
    )
    gram = lax.psum(
        jnp.einsum("dmk,dml->mkl", spanned, spanned, precision=lax.Precision.HIGHEST), "shard"
    )
    normalizer = norm_of(gram, (1, 2))
    oriented = spanned * normalizer[None, :, None]
    ortho_gram = gram * (normalizer * normalizer)[:, None, None]
    polished = 1.5 * oriented - 0.5 * jnp.einsum(
        "dmk,mkl->dml", oriented, ortho_gram, precision=lax.Precision.HIGHEST
    )
    return new_weights, new_one, new_two, (math.sqrt(D) * polished).astype(bf16)


def norm_of(gram, axes):
    return 1.7 / jnp.sqrt(jnp.sqrt(jnp.sum(gram * gram, axis=axes)) + 1e-06)


def adam(projected, one, two):
    new_one = 0.9 * one + 0.1 * projected
    new_two = 0.999 * two + 0.001 * projected * projected
    direction = new_one / first_fix / (jnp.sqrt(new_two / second_fix) + 1e-08)
    return new_one, new_two, direction.astype(bf16)


def swap(x, axis, bit, size):
    return lax.ppermute(x, axis, [(i, i ^ bit) for i in range(size)])


def pack_kernel(place_ref, x_ref, *refs):
    outs, sem = refs[:-1], refs[-1]
    copies = []
    for a in range(4):
        for l in range(2):
            for k in range(4):
                column = (
                    (jnp.bitwise_xor(place_ref[1], k) * 2 + jnp.bitwise_xor(place_ref[2], l)) * 4
                    + jnp.bitwise_xor(place_ref[0], a)
                ) * 128
                source = x_ref.at[:, :, pl.ds(pl.multiple_of(column, 128), 128)]
                copies.append(
                    pltpu.make_async_copy(source, outs[a].at[l * 4 + k], sem.at[len(copies)])
                )
    for copy in copies:
        copy.start()
    for copy in copies:
        copy.wait()


def pack(place, x):
    rows = x.shape[0]
    piece = jax.ShapeDtypeStruct((8, rows, 2, 128), bf16)
    return pl.pallas_call(
        pack_kernel,
        out_shape=(piece,) * 4,
        in_specs=[pl.BlockSpec(memory_space=pltpu.SMEM), pl.BlockSpec(memory_space=pl.ANY)],
        out_specs=(pl.BlockSpec(memory_space=pl.ANY),) * 4,
        scratch_shapes=[pltpu.SemaphoreType.DMA((32,))],
    )(place, x)


def project_kernel(a_ref, b_ref, c_ref, d_ref, s_ref, g_ref, p_ref):
    total = (a_ref[0].astype(f32) + b_ref[0].astype(f32)) + (
        c_ref[0].astype(f32) + d_ref[0].astype(f32)
    )
    gradient = total.astype(bf16)
    g_ref[0] = gradient
    p_ref[0] = lax.dot_general(
        gradient, s_ref[...], (((0,), (0,)), ((), ())), preferred_element_type=f32
    )


def project(pieces, masked):
    rows = pieces[0].shape[1]
    block = pl.BlockSpec((1, rows, 128), lambda i: (i, 0, 0))
    return pl.pallas_call(
        project_kernel,
        grid=(8,),
        in_specs=[block] * 4 + [pl.BlockSpec((rows, 512), lambda i: (0, 0))],
        out_specs=(block, pl.BlockSpec((1, 128, 512), lambda i: (i, 0, 0))),
        out_shape=(
            jax.ShapeDtypeStruct((8, rows, 128), bf16),
            jax.ShapeDtypeStruct((8, 128, 512), f32),
        ),
    )(*pieces, masked)


def span_kernel(g_ref, *refs):
    p_refs, out_ref = refs[:8], refs[8]
    rows = out_ref.shape[0]
    total = jnp.zeros((rows, 512), f32)
    for i in range(8):
        total += jnp.dot(g_ref[i], p_refs[i][...], preferred_element_type=f32)
    odd = lax.broadcasted_iota(jnp.int32, (rows, 256), 0) % 2 == 1
    out_ref[...] = jnp.where(odd, total[:, 256:], total[:, :256]).astype(bf16)


def span(gradient, pieces):
    rows = gradient.shape[1]
    return pl.pallas_call(
        span_kernel, out_shape=jax.ShapeDtypeStruct((rows, 256), bf16)
    )(gradient, *pieces)


def gram_kernel(place_ref, a_ref, b_ref, c_ref, d_ref, spanned_ref, own_ref, other_ref):
    spanned = (a_ref[...].astype(f32) + b_ref[...].astype(f32)) + (
        c_ref[...].astype(f32) + d_ref[...].astype(f32)
    )
    spanned_ref[...] = spanned
    parity = lax.broadcasted_iota(jnp.int32, spanned.shape, 0) % 2
    mine = jnp.where(parity == place_ref[2], spanned, 0.0)
    theirs = spanned - mine
    for part, out_ref in ((mine, own_ref), (theirs, other_ref)):
        out_ref[...] = lax.dot_general(
            part,
            part,
            (((0,), (0,)), ((), ())),
            preferred_element_type=f32,
            precision=lax.Precision.HIGHEST,
        )


def grams(place, parts):
    rows = parts[0].shape[0]
    square = jax.ShapeDtypeStruct((256, 256), f32)
    vmem = pl.BlockSpec(memory_space=pltpu.VMEM)
    return pl.pallas_call(
        gram_kernel,
        in_specs=[pl.BlockSpec(memory_space=pltpu.SMEM)] + [vmem] * 4,
        out_specs=(vmem,) * 3,
        out_shape=(jax.ShapeDtypeStruct((rows, 256), f32), square, square),
    )(place, *parts)


def polish_kernel(place_ref, spanned_ref, own_ref, other_ref, out_ref):
    spanned = spanned_ref[...]
    parity = lax.broadcasted_iota(jnp.int32, spanned.shape, 0) % 2
    mine = parity == place_ref[2]
    total = jnp.zeros_like(spanned)
    for chosen, gram_ref in ((mine, own_ref), (jnp.logical_not(mine), other_ref)):
        gram = gram_ref[...]
        normalizer = norm_of(gram, (0, 1))
        oriented = jnp.where(chosen, spanned, 0.0) * normalizer
        ortho = gram * (normalizer * normalizer)
        total += 1.5 * oriented - 0.5 * jnp.dot(
            oriented, ortho, preferred_element_type=f32, precision=lax.Precision.HIGHEST
        )
    out_ref[...] = (math.sqrt(D) * total).astype(bf16)


def polish(place, spanned, own, other):
    vmem = pl.BlockSpec(memory_space=pltpu.VMEM)
    return pl.pallas_call(
        polish_kernel,
        in_specs=[pl.BlockSpec(memory_space=pltpu.SMEM)] + [vmem] * 3,
        out_specs=vmem,
        out_shape=jax.ShapeDtypeStruct(spanned.shape, bf16),
    )(place, spanned, own, other)


def per_device(partials, weights, subspace, moment_one, moment_two):
    rows = weights.shape[0]
    g = lax.axis_index("grp")
    s = lax.axis_index("shard")
    z, c = s // 2, s % 2
    place = jnp.stack([g, z, c]).astype(jnp.int32)

    flat = subspace.reshape(2 * rows, 256)
    odd = lax.broadcasted_iota(jnp.int32, flat.shape, 0) % 2 == 1
    zero = jnp.zeros_like(flat)
    masked = jnp.concatenate([jnp.where(odd, zero, flat), jnp.where(odd, flat, zero)], axis=1)

    pieces = pack(place, partials[0])
    arrived = [pieces[0]] + [swap(pieces[a], "grp", a, 4) for a in (1, 2, 3)]
    gradient, part = project([p.reshape(8, 2 * rows, 128) for p in arrived], masked)

    kept = part[:4] + swap(part[4:].astype(bf16), "shard", 1, 8).astype(f32)
    sent = [swap(kept[k].astype(bf16), "shard", 2 * k, 8).astype(f32) for k in (1, 2, 3)]
    projected = ((kept[0] + sent[0]) + (sent[1] + sent[2])) * inv_root
    half = projected.astype(bf16)

    one = moment_one.reshape(512, 512)
    two = moment_two.reshape(512, 512)
    _, _, direction = adam(
        projected,
        lax.dynamic_slice_in_dim(one, g * 128, 128, 0),
        lax.dynamic_slice_in_dim(two, g * 128, 128, 0),
    )

    halves = [half] + [swap(half, "shard", 2 * k, 8) for k in (1, 2, 3)]
    directions = [direction] + [swap(direction, "shard", 2 * k, 8) for k in (1, 2, 3)]
    far_halves = [swap(h, "shard", 1, 8) for h in halves]

    partial_span = span(gradient, halves + far_halves)
    spans = [partial_span] + [swap(partial_span, "grp", a, 4) for a in (1, 2, 3)]
    spanned, own, other = grams(place, spans)
    own = own + swap(other, "shard", 1, 8)
    ship = own.astype(bf16)
    own = (own + swap(ship, "shard", 2, 8).astype(f32)) + (
        swap(ship, "shard", 4, 8).astype(f32) + swap(ship, "shard", 6, 8).astype(f32)
    )
    other = swap(own, "shard", 1, 8)
    new_subspace = polish(place, spanned, own, other).reshape(rows, 2, 256)

    gathered = [half] + [swap(half, "grp", a, 4) for a in (1, 2, 3)]
    block = jnp.zeros((4, 128, 512), bf16)
    for a in range(4):
        block = lax.dynamic_update_slice(block, gathered[a][None], (jnp.bitwise_xor(g, a), 0, 0))
    new_one, new_two, _ = adam(block.reshape(512, 512).astype(f32), one, two)

    stack = jnp.stack(directions)
    near = [stack] + [swap(stack, "grp", a, 4) for a in (1, 2, 3)]
    far = [swap(n, "shard", 1, 8) for n in near]
    full = jnp.zeros((4, 2, 4, 128, 512), bf16)
    for a in range(4):
        for l, held in ((0, near[a]), (1, far[a])):
            for k in range(4):
                full = lax.dynamic_update_slice(
                    full,
                    held[k][None, None, None],
                    (jnp.bitwise_xor(z, k), jnp.bitwise_xor(c, l), jnp.bitwise_xor(g, a), 0, 0),
                )
    full = full.reshape(4096, 2, 256)
    increment = jnp.einsum("dmk,fmk->dmf", subspace, full, preferred_element_type=f32)
    new_weights = weights - increment * inv_root
    return (
        new_weights,
        new_one.reshape(512, 2, 256),
        new_two.reshape(512, 2, 256),
        new_subspace,
    )


def solution(mesh):
    small = mesh.shape["grp"] == 4 and mesh.shape["shard"] == 8
    return jax.shard_map(
        per_device if small else plain,
        mesh=mesh,
        in_specs=(
            P("grp", "shard", None, None),
            P("shard", None, None),
            P("shard", None, None),
            P("shard", None, None),
            P("shard", None, None),
        ),
        out_specs=(
            P("shard", None, None),
            P("shard", None, None),
            P("shard", None, None),
            P("shard", None, None),
        ),
        check_vma=False,
    )
```

```python
import math

import jax
import jax.numpy as jnp
from jax import lax
from jax.experimental import pallas as pl
from jax.experimental.pallas import tpu as pltpu
from jax.sharding import PartitionSpec as P

D = 1536
bf16 = jnp.bfloat16
f32 = jnp.float32
inv_root = 1.0 / math.sqrt(D)
first_fix = 1.0 - 0.9**10
second_fix = 1.0 - 0.999**10


def plain(partials, weights, subspace, moment_one, moment_two):
    gradient = lax.psum(partials[0], "grp")
    projected = lax.psum_scatter(
        jnp.einsum("dmf,dmk->fmk", gradient, subspace, preferred_element_type=f32) * inv_root,
        "shard",
        scatter_dimension=0,
        tiled=True,
    )
    new_one, new_two, direction = adam(projected, moment_one, moment_two)
    increment = jnp.einsum(
        "dmk,fmk->dmf",
        subspace,
        lax.all_gather(direction, "shard", axis=0, tiled=True),
        preferred_element_type=f32,
    )
    new_weights = weights - increment * inv_root
    spanned = jnp.einsum(
        "dmf,fmk->dmk",
        gradient,
        lax.all_gather(projected.astype(bf16), "shard", axis=0, tiled=True),
        preferred_element_type=f32,
    )
    gram = lax.psum(
        jnp.einsum("dmk,dml->mkl", spanned, spanned, precision=lax.Precision.HIGHEST), "shard"
    )
    normalizer = norm_of(gram, (1, 2))
    oriented = spanned * normalizer[None, :, None]
    ortho_gram = gram * (normalizer * normalizer)[:, None, None]
    polished = 1.5 * oriented - 0.5 * jnp.einsum(
        "dmk,mkl->dml", oriented, ortho_gram, precision=lax.Precision.HIGHEST
    )
    return new_weights, new_one, new_two, (math.sqrt(D) * polished).astype(bf16)


def norm_of(gram, axes):
    return 1.7 / jnp.sqrt(jnp.sqrt(jnp.sum(gram * gram, axis=axes)) + 1e-06)


def adam(projected, one, two):
    new_one = 0.9 * one + 0.1 * projected
    new_two = 0.999 * two + 0.001 * projected * projected
    direction = new_one / first_fix / (jnp.sqrt(new_two / second_fix) + 1e-08)
    return new_one, new_two, direction.astype(bf16)


def swap(x, axis, bit, size):
    return lax.ppermute(x, axis, [(i, i ^ bit) for i in range(size)])


VMEM = pl.BlockSpec(memory_space=pltpu.VMEM)
SMEM = pl.BlockSpec(memory_space=pltpu.SMEM)
PARAMS = pltpu.CompilerParams(vmem_limit_bytes=24 * 2**20)
xor = jnp.bitwise_xor


def pin(x):
    return pltpu.with_memory_space_constraint(x, pltpu.VMEM)


def call(body, outs, *args, place=None):
    scalars = [] if place is None else [place]
    return pl.pallas_call(
        body,
        in_specs=[SMEM] * len(scalars) + [VMEM] * len(args),
        out_specs=(VMEM,) * len(outs),
        out_shape=tuple(pltpu.VMEM(shape, dtype) for shape, dtype in outs),
        compiler_params=PARAMS,
    )(*scalars, *[pin(a) for a in args])


def pack(place, x, a):
    rows = x.shape[0]

    def body(place_ref, x_ref, high_ref, low_ref):
        i = pl.program_id(0)
        piece = x_ref[...].reshape(2 * rows, 128)

        @pl.when(i < 4)
        def _():
            high_ref[i] = piece

        @pl.when(i >= 4)
        def _():
            low_ref[i - 4] = piece

    def where(i, place_ref):
        k, l = 2 * (1 - i // 4) + i % 2, i // 2 % 2
        shard = xor(place_ref[1], k) * 2 + xor(place_ref[2], l)
        return 0, 0, shard * 4 + xor(place_ref[0], a)

    half = pltpu.VMEM((4, 2 * rows, 128), bf16)
    whole = pl.BlockSpec(memory_space=pltpu.VMEM)
    return pl.pallas_call(
        body,
        grid_spec=pltpu.PrefetchScalarGridSpec(
            num_scalar_prefetch=1,
            grid=(8,),
            in_specs=[pl.BlockSpec((rows, 2, 128), where)],
            out_specs=(whole, whole),
        ),
        out_shape=(half, half),
        compiler_params=PARAMS,
    )(place, x)


def project(pieces, masked):
    rows = masked.shape[0]

    def body(a_ref, b_ref, c_ref, d_ref, s_ref, g_ref, keep_ref, send_ref):
        for i in (2, 3, 0, 1):
            total = (a_ref[i].astype(f32) + b_ref[i].astype(f32)) + (
                c_ref[i].astype(f32) + d_ref[i].astype(f32)
            )
            gradient = total.astype(bf16)
            g_ref[i] = gradient
            part = lax.dot_general(
                gradient, s_ref[...], (((0,), (0,)), ((), ())), preferred_element_type=f32
            )
            if i < 2:
                keep_ref[i] = part
            else:
                send_ref[i - 2] = part.astype(bf16)

    return call(
        body,
        [((4, rows, 128), bf16), ((2, 128, 512), f32), ((2, 128, 512), bf16)],
        *pieces,
        masked,
    )


def add_core(keep, came, first):
    def body(keep_ref, came_ref, a_ref, b_ref):
        a_ref[...] = (keep_ref[0] + came_ref[0].astype(f32)).astype(first)
        b_ref[...] = (keep_ref[1] + came_ref[1].astype(f32)).astype(bf16)

    return call(body, [((128, 512), first), ((128, 512), bf16)], keep, came)


def finish(parts):
    def body(a_ref, b_ref, c_ref, d_ref, half_ref):
        total = (a_ref[...] + b_ref[...].astype(f32)) + (
            c_ref[...].astype(f32) + d_ref[...].astype(f32)
        )
        half_ref[...] = (total * inv_root).astype(bf16)

    return call(body, [((128, 512), bf16)], *parts)[0]


def moments(place, gathered, one, two):
    def body(place_ref, a_ref, b_ref, c_ref, d_ref, one_ref, two_ref, new_one_ref, new_two_ref, own_ref, all_ref):
        for a, ref in enumerate((a_ref, b_ref, c_ref, d_ref)):
            at = pl.ds(pl.multiple_of(xor(place_ref[0], a) * 128, 128), 128)
            for m in range(2):
                lanes = slice(256 * m, 256 * (m + 1))
                projected = ref[:, lanes].astype(f32)
                new_one, new_two, direction = adam(projected, one_ref[at, m, :], two_ref[at, m, :])
                new_one_ref[at, m, :] = new_one
                new_two_ref[at, m, :] = new_two
                all_ref[a, :, lanes] = direction
                if a == 0:
                    own_ref[:, lanes] = direction

    return pl.pallas_call(
        body,
        in_specs=[SMEM] + [VMEM] * 6,
        out_specs=(VMEM,) * 4,
        out_shape=(
            jax.ShapeDtypeStruct(one.shape, f32),
            jax.ShapeDtypeStruct(one.shape, f32),
            pltpu.VMEM((128, 512), bf16),
            pltpu.VMEM((4, 128, 512), bf16),
        ),
        compiler_params=PARAMS,
    )(place, *[pin(x) for x in gathered], one, two)


def span(high, low, pieces):
    rows = high.shape[1]

    def body(high_ref, low_ref, *refs):
        p_refs, out_ref = refs[:8], refs[8]
        total = None
        for l in range(2):
            for k in range(4):
                g_ref = high_ref if k >= 2 else low_ref
                term = jnp.dot(
                    g_ref[l * 2 + k % 2], p_refs[l * 4 + k][...], preferred_element_type=f32
                )
                total = term if total is None else total + term
        odd = lax.broadcasted_iota(jnp.int32, (rows, 256), 0) % 2 == 1
        out_ref[...] = jnp.where(odd, total[:, 256:], total[:, :256]).astype(bf16)

    return call(body, [((rows, 256), bf16)], high, low, *pieces)[0]


def grams(place, parts):
    rows = parts[0].shape[0]

    def body(place_ref, a_ref, b_ref, c_ref, d_ref, spanned_ref, own_ref, other_ref):
        spanned = (a_ref[...].astype(f32) + b_ref[...].astype(f32)) + (
            c_ref[...].astype(f32) + d_ref[...].astype(f32)
        )
        spanned_ref[...] = spanned
        parity = lax.broadcasted_iota(jnp.int32, spanned.shape, 0) % 2
        mine = jnp.where(parity == place_ref[2], spanned, 0.0)
        theirs = jnp.where(parity == place_ref[2], 0.0, spanned)
        for part, out_ref in ((theirs, other_ref), (mine, own_ref)):
            out_ref[...] = lax.dot_general(
                part,
                part,
                (((0,), (0,)), ((), ())),
                preferred_element_type=f32,
                precision=lax.Precision.HIGHEST,
            )

    square = ((256, 256), f32)
    return call(body, [((rows, 256), f32), square, square], *parts, place=place)


def gram_core(own, came):
    def body(own_ref, came_ref, sum_ref, ship_ref):
        total = own_ref[...] + came_ref[...]
        sum_ref[...] = total
        ship_ref[...] = total.astype(bf16)

    return call(body, [((256, 256), f32), ((256, 256), bf16)], own, came)


def gram_chips(parts):
    def body(a_ref, b_ref, c_ref, d_ref, out_ref):
        out_ref[...] = (a_ref[...] + b_ref[...].astype(f32)) + (
            c_ref[...].astype(f32) + d_ref[...].astype(f32)
        )

    return call(body, [((256, 256), f32)], *parts)[0]


def polish(place, spanned, own, other):
    rows = spanned.shape[0]

    def body(place_ref, spanned_ref, own_ref, other_ref, out_ref):
        spanned = spanned_ref[...]
        parity = lax.broadcasted_iota(jnp.int32, spanned.shape, 0) % 2
        mine = parity == place_ref[2]
        total = jnp.zeros_like(spanned)
        for chosen, gram_ref in ((mine, own_ref), (jnp.logical_not(mine), other_ref)):
            gram = gram_ref[...]
            normalizer = norm_of(gram, (0, 1))
            oriented = jnp.where(chosen, spanned, 0.0) * normalizer
            ortho = gram * (normalizer * normalizer)
            total += 1.5 * oriented - 0.5 * jnp.dot(
                oriented, ortho, preferred_element_type=f32, precision=lax.Precision.HIGHEST
            )
        out_ref[...] = (math.sqrt(D) * total).astype(bf16)

    return call(body, [((rows, 256), bf16)], spanned, own, other, place=place)[0]


def update(place, weights, masked, held):
    rows = weights.shape[0]

    def body(place_ref, w_ref, s_ref, *refs):
        sides, out_ref = (refs[:7], refs[7:14]), refs[14]
        for i in range(8):
            l, k = i // 4, i % 4

            @pl.when(pl.program_id(0) == i)
            def _():
                side = sides[l]
                for a in range(4):
                    if k == 0:
                        piece = side[0][a]
                    elif a == 0:
                        piece = side[k][...]
                    else:
                        piece = side[3 + a][k - 1]
                    at = pl.ds(pl.multiple_of(xor(place_ref[0], a) * 128, 128), 128)
                    change = lax.dot_general(
                        s_ref[...], piece, (((1,), (1,)), ((), ())), preferred_element_type=f32
                    )
                    out_ref[:, :, at] = w_ref[:, :, at] - (change * inv_root).reshape(rows, 2, 128)

    def where(i, place_ref):
        return 0, 0, xor(place_ref[1], i % 4) * 2 + xor(place_ref[2], i // 4)

    block = pl.BlockSpec((rows, 2, 512), where)
    return pl.pallas_call(
        body,
        grid_spec=pltpu.PrefetchScalarGridSpec(
            num_scalar_prefetch=1,
            grid=(8,),
            in_specs=[block] + [VMEM] * 15,
            out_specs=block,
        ),
        out_shape=jax.ShapeDtypeStruct(weights.shape, f32),
        compiler_params=PARAMS,
    )(place, weights, pin(masked), *[pin(x) for x in held[0] + held[1]])


def per_device(partials, weights, subspace, moment_one, moment_two):
    rows = weights.shape[0]
    g = lax.axis_index("grp")
    s = lax.axis_index("shard")
    place = jnp.stack([g, s >> 1, s & 1]).astype(jnp.int32)

    def core(x):
        return swap(x, "shard", 1, 8)

    def chip(x, k):
        return swap(x, "shard", 2 * k, 8)

    def group(x, a):
        return swap(x, "grp", a, 4)

    flat = subspace.reshape(2 * rows, 256)
    odd = lax.broadcasted_iota(jnp.int32, flat.shape, 0) % 2 == 1
    zero = jnp.zeros_like(flat)
    masked = jnp.concatenate([jnp.where(odd, zero, flat), jnp.where(odd, flat, zero)], axis=1)

    packed = [pack(place, partials[0], a) for a in range(4)]
    high = [packed[0][0]] + [group(packed[a][0], a) for a in (1, 2, 3)]
    low = [packed[0][1]] + [group(packed[a][1], a) for a in (1, 2, 3)]

    gradient_high, keep, send = project(high, masked)
    q2, q3 = add_core(keep, core(send), bf16)
    r2, r3 = chip(q2, 2), chip(q3, 3)
    gradient_low, keep, send = project(low, masked)
    q0, q1 = add_core(keep, core(send), f32)
    half = finish([q0, chip(q1, 1), r2, r3])

    halves = [half] + [chip(half, k) for k in (1, 2, 3)]
    gathered = [half] + [group(half, a) for a in (1, 2, 3)]
    far_halves = [core(h) for h in halves]

    part = span(gradient_high, gradient_low, halves + far_halves)
    spanned, own, other = grams(place, [part] + [group(part, a) for a in (1, 2, 3)])
    own, ship = gram_core(own, core(other))
    own = gram_chips([own] + [chip(ship, k) for k in (1, 2, 3)])
    new_subspace = polish(place, spanned, own, core(own)).reshape(rows, 2, 256)

    new_one, new_two, mine, local = moments(place, gathered, moment_one, moment_two)
    along = [chip(mine, k) for k in (1, 2, 3)]
    stack = jnp.stack(along)
    near = [local] + along + [group(stack, a) for a in (1, 2, 3)]
    far = [core(x) for x in near]
    new_weights = update(place, weights, masked, (near, far))
    return new_weights, new_one, new_two, new_subspace


def solution(mesh):
    small = mesh.shape["grp"] == 4 and mesh.shape["shard"] == 8
    return jax.shard_map(
        per_device if small else plain,
        mesh=mesh,
        in_specs=(
            P("grp", "shard", None, None),
            P("shard", None, None),
            P("shard", None, None),
            P("shard", None, None),
            P("shard", None, None),
        ),
        out_specs=(
            P("shard", None, None),
            P("shard", None, None),
            P("shard", None, None),
            P("shard", None, None),
        ),
        check_vma=False,
    )
```

```python
import math

import jax
import jax.numpy as jnp
from jax import lax
from jax.experimental import pallas as pl
from jax.experimental.pallas import tpu as pltpu
from jax.sharding import PartitionSpec as P

D = 1536
bf16 = jnp.bfloat16
f32 = jnp.float32
inv_root = 1.0 / math.sqrt(D)
first_fix = 1.0 - 0.9**10
second_fix = 1.0 - 0.999**10


def plain(partials, weights, subspace, moment_one, moment_two):
    gradient = lax.psum(partials[0], "grp")
    projected = lax.psum_scatter(
        jnp.einsum("dmf,dmk->fmk", gradient, subspace, preferred_element_type=f32) * inv_root,
        "shard",
        scatter_dimension=0,
        tiled=True,
    )
    new_one, new_two, direction = adam(projected, moment_one, moment_two)
    increment = jnp.einsum(
        "dmk,fmk->dmf",
        subspace,
        lax.all_gather(direction, "shard", axis=0, tiled=True),
        preferred_element_type=f32,
    )
    new_weights = weights - increment * inv_root
    spanned = jnp.einsum(
        "dmf,fmk->dmk",
        gradient,
        lax.all_gather(projected.astype(bf16), "shard", axis=0, tiled=True),
        preferred_element_type=f32,
    )
    gram = lax.psum(
        jnp.einsum("dmk,dml->mkl", spanned, spanned, precision=lax.Precision.HIGHEST), "shard"
    )
    normalizer = norm_of(gram, (1, 2))
    oriented = spanned * normalizer[None, :, None]
    ortho_gram = gram * (normalizer * normalizer)[:, None, None]
    polished = 1.5 * oriented - 0.5 * jnp.einsum(
        "dmk,mkl->dml", oriented, ortho_gram, precision=lax.Precision.HIGHEST
    )
    return new_weights, new_one, new_two, (math.sqrt(D) * polished).astype(bf16)


def norm_of(gram, axes):
    return 1.7 / jnp.sqrt(jnp.sqrt(jnp.sum(gram * gram, axis=axes)) + 1e-06)


def adam(projected, one, two):
    new_one = 0.9 * one + 0.1 * projected
    new_two = 0.999 * two + 0.001 * projected * projected
    direction = new_one / first_fix / (jnp.sqrt(new_two / second_fix) + 1e-08)
    return new_one, new_two, direction.astype(bf16)


def swap(x, axis, bit, size):
    return lax.ppermute(x, axis, [(i, i ^ bit) for i in range(size)])


VMEM = pl.BlockSpec(memory_space=pltpu.VMEM)
SMEM = pl.BlockSpec(memory_space=pltpu.SMEM)
PARAMS = pltpu.CompilerParams(vmem_limit_bytes=16 * 2**20)
xor = jnp.bitwise_xor


def pin(x):
    return pltpu.with_memory_space_constraint(x, pltpu.VMEM)


def cost(us):
    return pl.CostEstimate(flops=0, transcendentals=0, bytes_accessed=int(us * 3.5e6))


def call(body, outs, *args, place=None, us=0.3):
    scalars = [] if place is None else [place]
    return pl.pallas_call(
        body,
        in_specs=[SMEM] * len(scalars) + [VMEM] * len(args),
        out_specs=(VMEM,) * len(outs),
        out_shape=tuple(pltpu.VMEM(shape, dtype) for shape, dtype in outs),
        compiler_params=PARAMS,
        cost_estimate=cost(us),
    )(*scalars, *[pin(a) for a in args])


def after(x, *others):
    return lax.optimization_barrier((x, others))[0]


def hbm(x):
    return pltpu.with_memory_space_constraint(x, pltpu.HBM)


def pack(place, x, half):
    rows = x.shape[0]

    def body(place_ref, x_ref, *out_refs):
        for a in range(4):
            at = pl.ds(pl.multiple_of(xor(place_ref[0], a) * 128, 128), 128)
            out_refs[a][pl.program_id(0)] = x_ref[:, :, at].reshape(2 * rows, 128)

    def where(i, place_ref):
        k, l = 2 * half + i % 2, i // 2
        return 0, 0, xor(place_ref[1], k) * 2 + xor(place_ref[2], l)

    return pl.pallas_call(
        body,
        grid_spec=pltpu.PrefetchScalarGridSpec(
            num_scalar_prefetch=1,
            grid=(4,),
            in_specs=[pl.BlockSpec((rows, 2, 512), where)],
            out_specs=(VMEM,) * 4,
        ),
        out_shape=(pltpu.VMEM((4, 2 * rows, 128), bf16),) * 4,
        compiler_params=PARAMS,
        cost_estimate=cost(3.3),
    )(place, hbm(x))


def project(pieces, masked, us):
    rows = masked.shape[0]

    def body(a_ref, b_ref, c_ref, d_ref, s_ref, g_ref, keep_ref, send_ref):
        for i in (2, 3, 0, 1):
            total = (a_ref[i].astype(f32) + b_ref[i].astype(f32)) + (
                c_ref[i].astype(f32) + d_ref[i].astype(f32)
            )
            gradient = total.astype(bf16)
            g_ref[i] = gradient
            part = lax.dot_general(
                gradient, s_ref[...], (((0,), (0,)), ((), ())), preferred_element_type=f32
            )
            if i < 2:
                keep_ref[i] = part
            else:
                send_ref[i - 2] = part.astype(bf16)

    return call(
        body,
        [((4, rows, 128), bf16), ((2, 128, 512), f32), ((2, 128, 512), bf16)],
        *pieces,
        masked,
        us=us,
    )


def add_core(keep, came, first):
    def body(keep_ref, came_ref, a_ref, b_ref):
        a_ref[...] = (keep_ref[0] + came_ref[0].astype(f32)).astype(first)
        b_ref[...] = (keep_ref[1] + came_ref[1].astype(f32)).astype(bf16)

    return call(body, [((128, 512), first), ((128, 512), bf16)], keep, came)


def finish(parts):
    def body(a_ref, b_ref, c_ref, d_ref, half_ref):
        total = (a_ref[...] + b_ref[...].astype(f32)) + (
            c_ref[...].astype(f32) + d_ref[...].astype(f32)
        )
        half_ref[...] = (total * inv_root).astype(bf16)

    return call(body, [((128, 512), bf16)], *parts)[0]


def own_direction(place, half, one, two):
    def body(place_ref, half_ref, one_ref, two_ref, own_ref):
        at = pl.ds(pl.multiple_of(place_ref[0] * 128, 128), 128)
        for m in range(2):
            lanes = slice(256 * m, 256 * (m + 1))
            projected = half_ref[:, lanes].astype(f32)
            own_ref[:, lanes] = adam(projected, one_ref[at, m, :], two_ref[at, m, :])[2]

    return call(body, [((128, 512), bf16)], half, one, two, place=place, us=0.9)[0]


def moments(place, gathered, one, two):
    def body(place_ref, *refs):
        halves, (one_ref, two_ref, new_one_ref, new_two_ref, all_ref) = refs[:4], refs[4:]
        for a in range(4):
            at = pl.ds(pl.multiple_of(xor(place_ref[0], a) * 128, 128), 128)
            for m in range(2):
                lanes = slice(256 * m, 256 * (m + 1))
                projected = halves[a][:, lanes].astype(f32)
                new_one, new_two, direction = adam(projected, one_ref[at, m, :], two_ref[at, m, :])
                new_one_ref[at, m, :] = new_one
                new_two_ref[at, m, :] = new_two
                all_ref[a, :, lanes] = direction

    return pl.pallas_call(
        body,
        in_specs=[SMEM] + [VMEM] * 6,
        out_specs=(VMEM,) * 3,
        out_shape=(
            jax.ShapeDtypeStruct(one.shape, f32),
            jax.ShapeDtypeStruct(one.shape, f32),
            pltpu.VMEM((4, 128, 512), bf16),
        ),
        compiler_params=PARAMS,
        cost_estimate=cost(3.5),
    )(place, *[pin(x) for x in gathered], one, two)


def span(high, low, pieces):
    rows = high.shape[1]

    def body(high_ref, low_ref, *refs):
        p_refs, out_ref = refs[:8], refs[8]
        total = None
        for l in range(2):
            for k in range(4):
                g_ref = high_ref if k >= 2 else low_ref
                term = jnp.dot(
                    g_ref[l * 2 + k % 2], p_refs[l * 4 + k][...], preferred_element_type=f32
                )
                total = term if total is None else total + term
        odd = lax.broadcasted_iota(jnp.int32, (rows, 256), 0) % 2 == 1
        out_ref[...] = jnp.where(odd, total[:, 256:], total[:, :256]).astype(bf16)

    return call(body, [((rows, 256), bf16)], high, low, *pieces, us=1.0)[0]


def grams(place, parts):
    rows = parts[0].shape[0]

    def body(place_ref, a_ref, b_ref, c_ref, d_ref, spanned_ref, own_ref, other_ref):
        spanned = (a_ref[...].astype(f32) + b_ref[...].astype(f32)) + (
            c_ref[...].astype(f32) + d_ref[...].astype(f32)
        )
        spanned_ref[...] = spanned
        parity = lax.broadcasted_iota(jnp.int32, spanned.shape, 0) % 2
        mine = jnp.where(parity == place_ref[2], spanned, 0.0)
        theirs = jnp.where(parity == place_ref[2], 0.0, spanned)
        for part, out_ref in ((theirs, other_ref), (mine, own_ref)):
            left, right = part[:, :128], part[:, 128:]
            for i, (x, y) in enumerate(((left, left), (left, right), (right, right))):
                out_ref[128 * i : 128 * (i + 1)] = lax.dot_general(
                    x,
                    y,
                    (((0,), (0,)), ((), ())),
                    preferred_element_type=f32,
                    precision=lax.Precision.HIGHEST,
                )

    blocks = ((384, 128), f32)
    return call(body, [((rows, 256), f32), blocks, blocks], *parts, place=place, us=1.8)


def gram_add(own, came):
    def body(own_ref, came_ref, sum_ref, ship_ref):
        total = own_ref[...] + came_ref[...].astype(f32)
        sum_ref[...] = total
        ship_ref[...] = total.astype(bf16)

    return call(body, [((384, 128), f32), ((384, 128), bf16)], own, came)


def polish(place, spanned, own, other):
    rows = spanned.shape[0]

    def body(place_ref, spanned_ref, own_ref, other_ref, out_ref):
        spanned = spanned_ref[...]
        parity = lax.broadcasted_iota(jnp.int32, spanned.shape, 0) % 2
        mine = parity == place_ref[2]
        total = jnp.zeros_like(spanned)
        for chosen, gram_ref in ((mine, own_ref), (jnp.logical_not(mine), other_ref)):
            a, b, d = gram_ref[:128], gram_ref[128:256], gram_ref[256:]
            squares = jnp.sum(a * a) + 2.0 * jnp.sum(b * b) + jnp.sum(d * d)
            normalizer = 1.7 / jnp.sqrt(jnp.sqrt(squares) + 1e-06)
            oriented = jnp.where(chosen, spanned, 0.0) * normalizer
            gram = jnp.concatenate(
                [jnp.concatenate([a, b], axis=1), jnp.concatenate([b.T, d], axis=1)], axis=0
            )
            total += 1.5 * oriented - 0.5 * jnp.dot(
                oriented,
                gram * (normalizer * normalizer),
                preferred_element_type=f32,
                precision=lax.Precision.HIGHEST,
            )
        out_ref[...] = (math.sqrt(D) * total).astype(bf16).reshape(rows // 2, 2, 256)

    return pl.pallas_call(
        body,
        in_specs=[SMEM] + [VMEM] * 3,
        out_specs=VMEM,
        out_shape=jax.ShapeDtypeStruct((rows // 2, 2, 256), bf16),
        compiler_params=PARAMS,
        cost_estimate=cost(1.8),
    )(place, pin(spanned), pin(own), pin(other))


def update(place, weights, masked, l0, ks, arrays, pieces, earlier):
    rows = weights.shape[0]
    steps = [(l, n) for l in range(len(pieces)) for n in range(len(ks))]

    def where(i, place_ref):
        k = ks[0] + i % len(ks)
        return 0, 0, xor(place_ref[1], k) * 2 + xor(place_ref[2], l0 + i // len(ks))

    def body(place_ref, w_ref, s_ref, *refs):
        held, out_ref, all_ref = refs[: len(arrays)], refs[-2], refs[-1]
        for i, (l, n) in enumerate(steps):

            @pl.when(pl.program_id(0) == i)
            def _():
                for a in range(4):
                    which, at, relative = pieces[l][n][a]
                    group = xor(place_ref[0], a) if relative else a
                    to = pl.ds(pl.multiple_of(group * 128, 128), 128)
                    all_ref[to] = held[which][at]

        change = lax.dot_general(
            s_ref[...], all_ref[...], (((1,), (1,)), ((), ())), preferred_element_type=f32
        )
        at = pl.ds(pl.multiple_of(where(pl.program_id(0), place_ref)[2] * 512, 512), 512)
        out_ref[...] = w_ref[:, :, at] - (change * inv_root).reshape(rows, 2, 512)

    before = [] if earlier is None else [earlier]
    return pl.pallas_call(
        body,
        grid_spec=pltpu.PrefetchScalarGridSpec(
            num_scalar_prefetch=1,
            grid=(len(steps),),
            in_specs=[VMEM] * (2 + len(arrays)) + [pl.BlockSpec(memory_space=pl.ANY)] * len(before),
            out_specs=pl.BlockSpec((rows, 2, 512), where),
            scratch_shapes=[pltpu.VMEM((512, 512), bf16)],
        ),
        out_shape=jax.ShapeDtypeStruct(weights.shape, f32),
        input_output_aliases={3 + len(arrays): 0} if before else {},
        compiler_params=PARAMS,
        cost_estimate=cost(0.5 + len(steps)),
    )(place, weights, pin(masked), *[pin(x) for x in arrays], *before)


def per_device(partials, weights, subspace, moment_one, moment_two):
    rows = weights.shape[0]
    g = lax.axis_index("grp")
    s = lax.axis_index("shard")
    place = jnp.stack([g, s >> 1, s & 1]).astype(jnp.int32)

    def core(x):
        return swap(x, "shard", 1, 8)

    def chip(x, k):
        return swap(x, "shard", 2 * k, 8)

    def group(x, a):
        return swap(x, "grp", a, 4)

    flat = subspace.reshape(2 * rows, 256)
    odd = lax.broadcasted_iota(jnp.int32, flat.shape, 0) % 2 == 1
    zero = jnp.zeros_like(flat)
    masked = jnp.concatenate([jnp.where(odd, zero, flat), jnp.where(odd, flat, zero)], axis=1)

    high = pack(place, partials[0], 1)
    low = pack(after(place, high), partials[0], 0)
    high = [high[0]] + [group(high[a], a) for a in (1, 2, 3)]
    low = [low[0]] + [group(after(low[a], high[1]), a) for a in (1, 2, 3)]

    gradient_high, keep, send = project(high, masked, 1.0)
    q2, q3 = add_core(keep, core(send), bf16)
    r2, r3 = chip(q2, 2), chip(q3, 3)
    low[3] = after(low[3], r2, r3)
    gradient_low, keep, send = project(low, masked, 1.0)
    q0, q1 = add_core(keep, core(send), f32)
    half = finish([q0, chip(q1, 1), r2, r3])

    gathered = [half] + [group(half, a) for a in (1, 2, 3)]
    late = after(half, gathered[1], gathered[2])
    halves = [half] + [chip(late if k == 1 else half, k) for k in (1, 2, 3)]
    far_half = core(late)
    mine = own_direction(place, half, moment_one, moment_two)

    new_one, new_two, local = moments(place, gathered, moment_one, moment_two)

    halves += [far_half] + [core(h) for h in halves[1:]]
    halves[0] = after(halves[0], gathered[3])
    part = span(gradient_high, gradient_low, halves)
    parts = [part] + [group(part, a) for a in (1, 2, 3)]
    mine = after(mine, part)
    along = [chip(mine, k) for k in (1, 2, 3)]
    spanned, own, other = grams(place, parts)
    own, ship = gram_add(own, core(other))
    own, ship = gram_add(own, chip(ship, 1))
    own, _ = gram_add(own, chip(ship, 2))
    new_subspace = polish(place, spanned, own, core(own))

    along = jnp.stack(along)
    held = [along] + [group(along, a) for a in (1, 2, 3)]
    weights = pin(weights)
    new_weights = update(
        place,
        weights,
        masked,
        0,
        (0,),
        [local, core(local)],
        [[[(l, a, True) for a in range(4)]] for l in range(2)],
        None,
    )
    held = after(held, new_weights, own)
    far = [core(x) for x in held]
    for l, side in ((0, held), (1, far)):
        new_weights = update(
            place,
            weights,
            masked,
            l,
            (1, 2, 3),
            side,
            [[[(a, n, True) for a in range(4)] for n in range(3)]],
            new_weights,
        )
    return new_weights, new_one, new_two, new_subspace


def solution(mesh):
    small = mesh.shape["grp"] == 4 and mesh.shape["shard"] == 8
    return jax.shard_map(
        per_device if small else plain,
        mesh=mesh,
        in_specs=(
            P("grp", "shard", None, None),
            P("shard", None, None),
            P("shard", None, None),
            P("shard", None, None),
            P("shard", None, None),
        ),
        out_specs=(
            P("shard", None, None),
            P("shard", None, None),
            P("shard", None, None),
            P("shard", None, None),
        ),
        check_vma=False,
    )
```

```python
import math

import jax
import jax.numpy as jnp
from jax import lax
from jax.experimental import pallas as pl
from jax.experimental.pallas import tpu as pltpu
from jax.sharding import PartitionSpec as P

D = 1536
bf16 = jnp.bfloat16
f32 = jnp.float32
inv_root = 1.0 / math.sqrt(D)
first_fix = 1.0 - 0.9**10
second_fix = 1.0 - 0.999**10


def plain(partials, weights, subspace, moment_one, moment_two):
    gradient = lax.psum(partials[0], "grp")
    projected = lax.psum_scatter(
        jnp.einsum("dmf,dmk->fmk", gradient, subspace, preferred_element_type=f32) * inv_root,
        "shard",
        scatter_dimension=0,
        tiled=True,
    )
    new_one, new_two, direction = adam(projected, moment_one, moment_two)
    increment = jnp.einsum(
        "dmk,fmk->dmf",
        subspace,
        lax.all_gather(direction, "shard", axis=0, tiled=True),
        preferred_element_type=f32,
    )
    new_weights = weights - increment * inv_root
    spanned = jnp.einsum(
        "dmf,fmk->dmk",
        gradient,
        lax.all_gather(projected.astype(bf16), "shard", axis=0, tiled=True),
        preferred_element_type=f32,
    )
    gram = lax.psum(
        jnp.einsum("dmk,dml->mkl", spanned, spanned, precision=lax.Precision.HIGHEST), "shard"
    )
    normalizer = norm_of(gram, (1, 2))
    oriented = spanned * normalizer[None, :, None]
    ortho_gram = gram * (normalizer * normalizer)[:, None, None]
    polished = 1.5 * oriented - 0.5 * jnp.einsum(
        "dmk,mkl->dml", oriented, ortho_gram, precision=lax.Precision.HIGHEST
    )
    return new_weights, new_one, new_two, (math.sqrt(D) * polished).astype(bf16)


def norm_of(gram, axes):
    return 1.7 / jnp.sqrt(jnp.sqrt(jnp.sum(gram * gram, axis=axes)) + 1e-06)


def adam(projected, one, two):
    new_one = 0.9 * one + 0.1 * projected
    new_two = 0.999 * two + 0.001 * projected * projected
    direction = new_one / first_fix / (jnp.sqrt(new_two / second_fix) + 1e-08)
    return new_one, new_two, direction.astype(bf16)


def swap(x, axis, bit, size):
    return lax.ppermute(x, axis, [(i, i ^ bit) for i in range(size)])


VMEM = pl.BlockSpec(memory_space=pltpu.VMEM)
SMEM = pl.BlockSpec(memory_space=pltpu.SMEM)
PARAMS = pltpu.CompilerParams(vmem_limit_bytes=16 * 2**20)
xor = jnp.bitwise_xor


def pin(x):
    return pltpu.with_memory_space_constraint(x, pltpu.VMEM)


def cost(us):
    return pl.CostEstimate(flops=0, transcendentals=0, bytes_accessed=int(us * 3.5e6))


def call(body, outs, *args, place=None, us=0.3):
    scalars = [] if place is None else [place]
    return pl.pallas_call(
        body,
        in_specs=[SMEM] * len(scalars) + [VMEM] * len(args),
        out_specs=(VMEM,) * len(outs),
        out_shape=tuple(pltpu.VMEM(shape, dtype) for shape, dtype in outs),
        compiler_params=PARAMS,
        cost_estimate=cost(us),
    )(*scalars, *[pin(a) for a in args])


def after(x, *others):
    return lax.optimization_barrier((x, others))[0]


def hbm(x):
    return pltpu.with_memory_space_constraint(x, pltpu.HBM)


def pack(place, x, half):
    rows = x.shape[0]

    def body(place_ref, x_ref, *out_refs):
        i = pl.program_id(0)
        for l, order in ((0, (1, 3, 0, 2)), (1, (2, 3, 0, 1))):

            @pl.when(i // 2 == l)
            def _():
                for n, a in enumerate(order):
                    at = pl.ds(pl.multiple_of(xor(place_ref[0], a) * 128, 128), 128)
                    out_refs[l + n // 2 * 2][n % 2, i % 2] = x_ref[:, :, at].reshape(2 * rows, 128)

    def where(i, place_ref):
        k, l = 2 * half + i % 2, i // 2
        return 0, 0, xor(place_ref[1], k) * 2 + xor(place_ref[2], l)

    return pl.pallas_call(
        body,
        grid_spec=pltpu.PrefetchScalarGridSpec(
            num_scalar_prefetch=1,
            grid=(4,),
            in_specs=[pl.BlockSpec((rows, 2, 512), where)],
            out_specs=(VMEM,) * 4,
        ),
        out_shape=(pltpu.VMEM((2, 2, 2 * rows, 128), bf16),) * 4,
        compiler_params=PARAMS,
        cost_estimate=cost(3.3),
    )(place, hbm(x))


def pair(stay_x, stay_y, came_x, came_y):
    def body(stay_x_ref, stay_y_ref, came_x_ref, came_y_ref, x_ref, y_ref):
        x_ref[...] = (stay_x_ref[1].astype(f32) + came_x_ref[1].astype(f32)).astype(bf16)
        y_ref[...] = (stay_y_ref[1].astype(f32) + came_y_ref[1].astype(f32)).astype(bf16)

    out = (stay_x.shape[1:], bf16)
    return call(body, [out, out], stay_x, stay_y, came_x, came_y)


def project(held, masked):
    rows = masked.shape[0]

    def body(*refs):
        sides, (s_ref, g_ref, keep_ref, send_ref) = (refs[:3], refs[3:6]), refs[6:]
        for i in (2, 3, 0, 1):
            stay, came, last = sides[i // 2]
            total = (stay[0, i % 2].astype(f32) + came[0, i % 2].astype(f32)) + last[i % 2].astype(
                f32
            )
            gradient = total.astype(bf16)
            g_ref[i] = gradient
            part = lax.dot_general(
                gradient, s_ref[...], (((0,), (0,)), ((), ())), preferred_element_type=f32
            )
            if i < 2:
                keep_ref[i] = part
            else:
                send_ref[i - 2] = part.astype(bf16)

    return call(
        body,
        [((4, rows, 128), bf16), ((2, 128, 512), f32), ((2, 128, 512), bf16)],
        *held,
        masked,
        us=0.01,
    )


def add_core(keep, came):
    def body(keep_ref, came_ref, out_ref):
        out_ref[...] = (keep_ref[...] + came_ref[...].astype(f32)).astype(bf16)

    return call(body, [((2, 128, 512), bf16)], keep, came)[0]


def add_chip(keep, came, chips):
    def body(keep_ref, came_ref, chips_ref, own_ref, next_ref):
        total = keep_ref[...] + came_ref[...].astype(f32) + chips_ref[...].astype(f32)
        own_ref[...] = total[0]
        next_ref[...] = total[1].astype(bf16)

    return call(body, [((128, 512), f32), ((128, 512), bf16)], keep, came, chips)


def finish(own, came):
    def body(own_ref, came_ref, half_ref):
        half_ref[...] = ((own_ref[...] + came_ref[...].astype(f32)) * inv_root).astype(bf16)

    return call(body, [((128, 512), bf16)], own, came)[0]


def own_direction(place, half, one, two):
    def body(place_ref, half_ref, one_ref, two_ref, own_ref):
        at = pl.ds(pl.multiple_of(place_ref[0] * 128, 128), 128)
        for m in range(2):
            lanes = slice(256 * m, 256 * (m + 1))
            projected = half_ref[:, lanes].astype(f32)
            own_ref[:, lanes] = adam(projected, one_ref[at, m, :], two_ref[at, m, :])[2]

    return call(body, [((128, 512), bf16)], half, one, two, place=place, us=0.9)[0]


def moments(place, gathered, one, two):
    def body(place_ref, *refs):
        halves, (one_ref, two_ref, new_one_ref, new_two_ref, all_ref) = refs[:4], refs[4:]
        for a in range(4):
            at = pl.ds(pl.multiple_of(xor(place_ref[0], a) * 128, 128), 128)
            for m in range(2):
                lanes = slice(256 * m, 256 * (m + 1))
                projected = halves[a][:, lanes].astype(f32)
                new_one, new_two, direction = adam(projected, one_ref[at, m, :], two_ref[at, m, :])
                new_one_ref[at, m, :] = new_one
                new_two_ref[at, m, :] = new_two
                all_ref[a, :, lanes] = direction

    return pl.pallas_call(
        body,
        in_specs=[SMEM] + [VMEM] * 6,
        out_specs=(VMEM,) * 3,
        out_shape=(
            jax.ShapeDtypeStruct(one.shape, f32),
            jax.ShapeDtypeStruct(one.shape, f32),
            pltpu.VMEM((4, 128, 512), bf16),
        ),
        compiler_params=PARAMS,
        cost_estimate=cost(3.5),
    )(place, *[pin(x) for x in gathered], one, two)


def span(high, low, pieces):
    rows = high.shape[1]

    def body(high_ref, low_ref, *refs):
        p_refs, out_ref = refs[:8], refs[8]
        total = None
        for l in range(2):
            for k in range(4):
                g_ref = high_ref if k >= 2 else low_ref
                term = jnp.dot(
                    g_ref[l * 2 + k % 2], p_refs[l * 4 + k][...], preferred_element_type=f32
                )
                total = term if total is None else total + term
        odd = lax.broadcasted_iota(jnp.int32, (rows, 256), 0) % 2 == 1
        out_ref[...] = jnp.where(odd, total[:, 256:], total[:, :256]).astype(bf16)

    return call(body, [((rows, 256), bf16)], high, low, *pieces, us=1.0)[0]


def grams(place, parts):
    rows = parts[0].shape[0]

    def body(place_ref, a_ref, b_ref, c_ref, d_ref, spanned_ref, own_ref, other_ref):
        spanned = (a_ref[...].astype(f32) + b_ref[...].astype(f32)) + (
            c_ref[...].astype(f32) + d_ref[...].astype(f32)
        )
        spanned_ref[...] = spanned
        parity = lax.broadcasted_iota(jnp.int32, spanned.shape, 0) % 2
        mine = jnp.where(parity == place_ref[2], spanned, 0.0)
        theirs = jnp.where(parity == place_ref[2], 0.0, spanned)
        for part, out_ref in ((theirs, other_ref), (mine, own_ref)):
            left, right = part[:, :128], part[:, 128:]
            for i, (x, y) in enumerate(((left, left), (left, right), (right, right))):
                out_ref[128 * i : 128 * (i + 1)] = lax.dot_general(
                    x,
                    y,
                    (((0,), (0,)), ((), ())),
                    preferred_element_type=f32,
                    precision=lax.Precision.HIGHEST,
                )

    blocks = ((384, 128), f32)
    return call(body, [((rows, 256), f32), blocks, blocks], *parts, place=place, us=1.8)


def gram_add(own, came):
    def body(own_ref, came_ref, sum_ref, ship_ref):
        total = own_ref[...] + came_ref[...].astype(f32)
        sum_ref[...] = total
        ship_ref[...] = total.astype(bf16)

    return call(body, [((384, 128), f32), ((384, 128), bf16)], own, came)


def polish(place, spanned, own, other):
    rows = spanned.shape[0]

    def body(place_ref, spanned_ref, own_ref, other_ref, out_ref):
        spanned = spanned_ref[...]
        parity = lax.broadcasted_iota(jnp.int32, spanned.shape, 0) % 2
        mine = parity == place_ref[2]
        total = jnp.zeros_like(spanned)
        for chosen, gram_ref in ((mine, own_ref), (jnp.logical_not(mine), other_ref)):
            a, b, d = gram_ref[:128], gram_ref[128:256], gram_ref[256:]
            squares = jnp.sum(a * a) + 2.0 * jnp.sum(b * b) + jnp.sum(d * d)
            normalizer = 1.7 / jnp.sqrt(jnp.sqrt(squares) + 1e-06)
            oriented = jnp.where(chosen, spanned, 0.0) * normalizer
            gram = jnp.concatenate(
                [jnp.concatenate([a, b], axis=1), jnp.concatenate([b.T, d], axis=1)], axis=0
            )
            total += 1.5 * oriented - 0.5 * jnp.dot(
                oriented,
                gram * (normalizer * normalizer),
                preferred_element_type=f32,
                precision=lax.Precision.HIGHEST,
            )
        out_ref[...] = (math.sqrt(D) * total).astype(bf16).reshape(rows // 2, 2, 256)

    return pl.pallas_call(
        body,
        in_specs=[SMEM] + [VMEM] * 3,
        out_specs=VMEM,
        out_shape=jax.ShapeDtypeStruct((rows // 2, 2, 256), bf16),
        compiler_params=PARAMS,
        cost_estimate=cost(1.8),
    )(place, pin(spanned), pin(own), pin(other))


def update(place, weights, masked, l0, ks, arrays, pieces, earlier):
    rows = weights.shape[0]
    steps = [(l, n) for l in range(len(pieces)) for n in range(len(ks))]

    def where(i, place_ref):
        k = ks[0] + i % len(ks)
        return 0, 0, xor(place_ref[1], k) * 2 + xor(place_ref[2], l0 + i // len(ks))

    def body(place_ref, w_ref, s_ref, *refs):
        held, out_ref, all_ref = refs[: len(arrays)], refs[-2], refs[-1]
        for i, (l, n) in enumerate(steps):

            @pl.when(pl.program_id(0) == i)
            def _():
                for a in range(4):
                    which, at, relative = pieces[l][n][a]
                    group = xor(place_ref[0], a) if relative else a
                    to = pl.ds(pl.multiple_of(group * 128, 128), 128)
                    all_ref[to] = held[which][at]

        change = lax.dot_general(
            s_ref[...], all_ref[...], (((1,), (1,)), ((), ())), preferred_element_type=f32
        )
        at = pl.ds(pl.multiple_of(where(pl.program_id(0), place_ref)[2] * 512, 512), 512)
        out_ref[...] = w_ref[:, :, at] - (change * inv_root).reshape(rows, 2, 512)

    before = [] if earlier is None else [earlier]
    return pl.pallas_call(
        body,
        grid_spec=pltpu.PrefetchScalarGridSpec(
            num_scalar_prefetch=1,
            grid=(len(steps),),
            in_specs=[VMEM] * (2 + len(arrays)) + [pl.BlockSpec(memory_space=pl.ANY)] * len(before),
            out_specs=pl.BlockSpec((rows, 2, 512), where),
            scratch_shapes=[pltpu.VMEM((512, 512), bf16)],
        ),
        out_shape=jax.ShapeDtypeStruct(weights.shape, f32),
        input_output_aliases={3 + len(arrays): 0} if before else {},
        compiler_params=PARAMS,
        cost_estimate=cost(0.5 + len(steps)),
    )(place, weights, pin(masked), *[pin(x) for x in arrays], *before)


def per_device(partials, weights, subspace, moment_one, moment_two):
    rows = weights.shape[0]
    g = lax.axis_index("grp")
    s = lax.axis_index("shard")
    place = jnp.stack([g, s >> 1, s & 1]).astype(jnp.int32)

    def core(x):
        return swap(x, "shard", 1, 8)

    def chip(x, k):
        return swap(x, "shard", 2 * k, 8)

    def group(x, a):
        return swap(x, "grp", a, 4)

    flat = subspace.reshape(2 * rows, 256)
    odd = lax.broadcasted_iota(jnp.int32, flat.shape, 0) % 2 == 1
    zero = jnp.zeros_like(flat)
    masked = jnp.concatenate([jnp.where(odd, zero, flat), jnp.where(odd, flat, zero)], axis=1)

    high = pack(place, partials[0], 1)
    low = pack(after(place, high), partials[0], 0)

    def over_groups(x, y, stay_x, stay_y):
        came_x, came_y = group(x, 1), group(y, 2)
        sum_x, sum_y = pair(stay_x, stay_y, came_x, came_y)
        return [stay_x, came_x, group(sum_x, 2), stay_y, came_y, group(sum_y, 1)]

    high = over_groups(high[0], high[1], after(high[2], low), high[3])
    low = over_groups(*after(low[:2], high[1], high[4]), *low[2:])

    gradient_high, keep, send = project(high, masked)
    chips = chip(add_core(keep, core(send)), 2)
    gradient_low, keep, send = project(low, masked)
    own, following = add_chip(keep, core(after(send, chips)), chips)
    half = finish(own, chip(following, 1))

    gathered = [half] + [group(half, a) for a in (1, 2, 3)]
    late = after(half, gathered[1], gathered[2])
    halves = [half] + [chip(late if k == 1 else half, k) for k in (1, 2, 3)]
    far_half = core(late)
    mine = own_direction(place, half, moment_one, moment_two)

    new_one, new_two, local = moments(place, gathered, moment_one, moment_two)

    halves += [far_half] + [core(h) for h in halves[1:]]
    halves[0] = after(halves[0], gathered[3])
    part = span(gradient_high, gradient_low, halves)
    parts = [part] + [group(part, a) for a in (1, 2, 3)]
    mine = after(mine, part)
    along = [chip(mine, k) for k in (1, 2, 3)]
    spanned, own, other = grams(place, parts)
    own, ship = gram_add(own, core(other))
    own, ship = gram_add(own, chip(ship, 1))
    own, _ = gram_add(own, chip(ship, 2))
    new_subspace = polish(place, spanned, own, core(own))

    along = jnp.stack(along)
    held = [along] + [group(along, a) for a in (1, 2, 3)]
    weights = pin(weights)
    new_weights = update(
        place,
        weights,
        masked,
        0,
        (0,),
        [local, core(local)],
        [[[(l, a, True) for a in range(4)]] for l in range(2)],
        None,
    )
    held = after(held, new_weights, own)
    far = [core(x) for x in held]
    for l, side in ((0, held), (1, far)):
        new_weights = update(
            place,
            weights,
            masked,
            l,
            (1, 2, 3),
            side,
            [[[(a, n, True) for a in range(4)] for n in range(3)]],
            new_weights,
        )
    return new_weights, new_one, new_two, new_subspace


def solution(mesh):
    small = mesh.shape["grp"] == 4 and mesh.shape["shard"] == 8
    return jax.shard_map(
        per_device if small else plain,
        mesh=mesh,
        in_specs=(
            P("grp", "shard", None, None),
            P("shard", None, None),
            P("shard", None, None),
            P("shard", None, None),
            P("shard", None, None),
        ),
        out_specs=(
            P("shard", None, None),
            P("shard", None, None),
            P("shard", None, None),
            P("shard", None, None),
        ),
        check_vma=False,
    )
```

```python
import math

import jax
import jax.numpy as jnp
from jax import lax
from jax.experimental import pallas as pl
from jax.experimental.pallas import tpu as pltpu
from jax.sharding import PartitionSpec as P

D = 1536
bf16 = jnp.bfloat16
f32 = jnp.float32
inv_root = 1.0 / math.sqrt(D)
first_fix = 1.0 - 0.9**10
second_fix = 1.0 - 0.999**10


def plain(partials, weights, subspace, moment_one, moment_two):
    gradient = lax.psum(partials[0], "grp")
    projected = lax.psum_scatter(
        jnp.einsum("dmf,dmk->fmk", gradient, subspace, preferred_element_type=f32) * inv_root,
        "shard",
        scatter_dimension=0,
        tiled=True,
    )
    new_one, new_two, direction = adam(projected, moment_one, moment_two)
    increment = jnp.einsum(
        "dmk,fmk->dmf",
        subspace,
        lax.all_gather(direction, "shard", axis=0, tiled=True),
        preferred_element_type=f32,
    )
    new_weights = weights - increment * inv_root
    spanned = jnp.einsum(
        "dmf,fmk->dmk",
        gradient,
        lax.all_gather(projected.astype(bf16), "shard", axis=0, tiled=True),
        preferred_element_type=f32,
    )
    gram = lax.psum(
        jnp.einsum("dmk,dml->mkl", spanned, spanned, precision=lax.Precision.HIGHEST), "shard"
    )
    normalizer = norm_of(gram, (1, 2))
    oriented = spanned * normalizer[None, :, None]
    ortho_gram = gram * (normalizer * normalizer)[:, None, None]
    polished = 1.5 * oriented - 0.5 * jnp.einsum(
        "dmk,mkl->dml", oriented, ortho_gram, precision=lax.Precision.HIGHEST
    )
    return new_weights, new_one, new_two, (math.sqrt(D) * polished).astype(bf16)


def norm_of(gram, axes):
    return 1.7 / jnp.sqrt(jnp.sqrt(jnp.sum(gram * gram, axis=axes)) + 1e-06)


def adam(projected, one, two):
    new_one = 0.9 * one + 0.1 * projected
    new_two = 0.999 * two + 0.001 * projected * projected
    direction = new_one / first_fix / (jnp.sqrt(new_two / second_fix) + 1e-08)
    return new_one, new_two, direction.astype(bf16)


def swap(x, axis, bit, size):
    return lax.ppermute(x, axis, [(i, i ^ bit) for i in range(size)])


VMEM = pl.BlockSpec(memory_space=pltpu.VMEM)
SMEM = pl.BlockSpec(memory_space=pltpu.SMEM)
PARAMS = pltpu.CompilerParams(vmem_limit_bytes=16 * 2**20)
xor = jnp.bitwise_xor


def pin(x):
    return pltpu.with_memory_space_constraint(x, pltpu.VMEM)


def cost(us):
    return pl.CostEstimate(flops=0, transcendentals=0, bytes_accessed=int(us * 3.5e6))


def call(body, outs, *args, place=None, us=0.3):
    scalars = [] if place is None else [place]
    return pl.pallas_call(
        body,
        in_specs=[SMEM] * len(scalars) + [VMEM] * len(args),
        out_specs=(VMEM,) * len(outs),
        out_shape=tuple(pltpu.VMEM(shape, dtype) for shape, dtype in outs),
        compiler_params=PARAMS,
        cost_estimate=cost(us),
    )(*scalars, *[pin(a) for a in args])


def after(x, *others):
    return lax.optimization_barrier((x, others))[0]


def hbm(x):
    return pltpu.with_memory_space_constraint(x, pltpu.HBM)


def pack(place, x, half):
    rows = x.shape[0]

    def body(place_ref, x_ref, *out_refs):
        i = pl.program_id(0)
        for l, order in ((0, (1, 3, 0, 2)), (1, (2, 3, 0, 1))):

            @pl.when(i // 2 == l)
            def _():
                for n, a in enumerate(order):
                    at = pl.ds(pl.multiple_of(xor(place_ref[0], a) * 128, 128), 128)
                    out_refs[l + n // 2 * 2][n % 2, i % 2] = x_ref[:, :, at].reshape(2 * rows, 128)

    def where(i, place_ref):
        k, l = 2 * half + i % 2, i // 2
        return 0, 0, xor(place_ref[1], k) * 2 + xor(place_ref[2], l)

    return pl.pallas_call(
        body,
        grid_spec=pltpu.PrefetchScalarGridSpec(
            num_scalar_prefetch=1,
            grid=(4,),
            in_specs=[pl.BlockSpec((rows, 2, 512), where)],
            out_specs=(VMEM,) * 4,
        ),
        out_shape=(pltpu.VMEM((2, 2, 2 * rows, 128), bf16),) * 4,
        compiler_params=PARAMS,
        cost_estimate=cost(3.3),
    )(place, hbm(x))


def pair(stay_x, stay_y, came_x, came_y):
    def body(stay_x_ref, stay_y_ref, came_x_ref, came_y_ref, x_ref, y_ref):
        x_ref[...] = (stay_x_ref[1].astype(f32) + came_x_ref[1].astype(f32)).astype(bf16)
        y_ref[...] = (stay_y_ref[1].astype(f32) + came_y_ref[1].astype(f32)).astype(bf16)

    out = (stay_x.shape[1:], bf16)
    return call(body, [out, out], stay_x, stay_y, came_x, came_y)


def project(held, masked):
    rows = masked.shape[0]

    def body(*refs):
        sides, (s_ref, g_ref, keep_ref, send_ref) = (refs[:3], refs[3:6]), refs[6:]
        for i in (2, 3, 0, 1):
            stay, came, last = sides[i // 2]
            total = (stay[0, i % 2].astype(f32) + came[0, i % 2].astype(f32)) + last[i % 2].astype(
                f32
            )
            gradient = total.astype(bf16)
            g_ref[i] = gradient
            part = lax.dot_general(
                gradient, s_ref[...], (((0,), (0,)), ((), ())), preferred_element_type=f32
            )
            if i < 2:
                keep_ref[i] = part
            else:
                send_ref[i - 2] = part.astype(bf16)

    return call(
        body,
        [((4, rows, 128), bf16), ((2, 128, 512), f32), ((2, 128, 512), bf16)],
        *held,
        masked,
        us=0.01,
    )


def add_core(keep, came):
    def body(keep_ref, came_ref, out_ref):
        out_ref[...] = (keep_ref[...] + came_ref[...].astype(f32)).astype(bf16)

    return call(body, [((2, 128, 512), bf16)], keep, came)[0]


def add_chip(keep, came, chips):
    def body(keep_ref, came_ref, chips_ref, own_ref, next_ref):
        total = keep_ref[...] + came_ref[...].astype(f32) + chips_ref[...].astype(f32)
        own_ref[...] = total[0]
        next_ref[...] = total[1].astype(bf16)

    return call(body, [((128, 512), f32), ((128, 512), bf16)], keep, came, chips)


def finish(own, came):
    def body(own_ref, came_ref, half_ref):
        half_ref[...] = ((own_ref[...] + came_ref[...].astype(f32)) * inv_root).astype(bf16)

    return call(body, [((128, 512), bf16)], own, came)[0]


def own_direction(place, half, one, two):
    def body(place_ref, half_ref, one_ref, two_ref, own_ref):
        at = pl.ds(pl.multiple_of(place_ref[0] * 128, 128), 128)
        for m in range(2):
            lanes = slice(256 * m, 256 * (m + 1))
            projected = half_ref[:, lanes].astype(f32)
            own_ref[:, lanes] = adam(projected, one_ref[at, m, :], two_ref[at, m, :])[2]

    return call(body, [((128, 512), bf16)], half, one, two, place=place, us=0.9)[0]


def moments(place, gathered, one, two):
    def body(place_ref, *refs):
        halves, (one_ref, two_ref, new_one_ref, new_two_ref, all_ref) = refs[:4], refs[4:]
        for a in range(4):
            at = pl.ds(pl.multiple_of(xor(place_ref[0], a) * 128, 128), 128)
            for m in range(2):
                lanes = slice(256 * m, 256 * (m + 1))
                projected = halves[a][:, lanes].astype(f32)
                new_one, new_two, direction = adam(projected, one_ref[at, m, :], two_ref[at, m, :])
                new_one_ref[at, m, :] = new_one
                new_two_ref[at, m, :] = new_two
                all_ref[a, :, lanes] = direction

    return pl.pallas_call(
        body,
        in_specs=[SMEM] + [VMEM] * 6,
        out_specs=(VMEM,) * 3,
        out_shape=(
            jax.ShapeDtypeStruct(one.shape, f32),
            jax.ShapeDtypeStruct(one.shape, f32),
            pltpu.VMEM((4, 128, 512), bf16),
        ),
        compiler_params=PARAMS,
        cost_estimate=cost(3.5),
    )(place, *[pin(x) for x in gathered], one, two)


def span(high, low, pieces):
    rows = high.shape[1]

    def body(high_ref, low_ref, *refs):
        p_refs, out_ref = refs[:8], refs[8]
        total = None
        for l in range(2):
            for k in range(4):
                g_ref = high_ref if k >= 2 else low_ref
                term = jnp.dot(
                    g_ref[l * 2 + k % 2], p_refs[l * 4 + k][...], preferred_element_type=f32
                )
                total = term if total is None else total + term
        odd = lax.broadcasted_iota(jnp.int32, (rows, 256), 0) % 2 == 1
        out_ref[...] = jnp.where(odd, total[:, 256:], total[:, :256]).astype(bf16)

    return call(body, [((rows, 256), bf16)], high, low, *pieces, us=1.0)[0]


def grams(place, parts):
    rows = parts[0].shape[0]

    def body(place_ref, a_ref, b_ref, c_ref, d_ref, spanned_ref, own_ref, other_ref):
        spanned = (a_ref[...].astype(f32) + b_ref[...].astype(f32)) + (
            c_ref[...].astype(f32) + d_ref[...].astype(f32)
        )
        spanned_ref[...] = spanned
        parity = lax.broadcasted_iota(jnp.int32, spanned.shape, 0) % 2
        mine = jnp.where(parity == place_ref[2], spanned, 0.0)
        theirs = jnp.where(parity == place_ref[2], 0.0, spanned)
        for part, out_ref in ((theirs, other_ref), (mine, own_ref)):
            left, right = part[:, :128], part[:, 128:]
            for i, (x, y) in enumerate(((left, left), (left, right), (right, right))):
                out_ref[128 * i : 128 * (i + 1)] = lax.dot_general(
                    x,
                    y,
                    (((0,), (0,)), ((), ())),
                    preferred_element_type=f32,
                    precision=lax.Precision.HIGHEST,
                )

    blocks = ((384, 128), f32)
    return call(body, [((rows, 256), f32), blocks, blocks], *parts, place=place, us=1.8)


def gram_add(own, came):
    def body(own_ref, came_ref, sum_ref, ship_ref):
        total = own_ref[...] + came_ref[...].astype(f32)
        sum_ref[...] = total
        ship_ref[...] = total.astype(bf16)

    return call(body, [((384, 128), f32), ((384, 128), bf16)], own, came)


def polish(place, spanned, own, other):
    rows = spanned.shape[0]

    def body(place_ref, spanned_ref, own_ref, other_ref, out_ref):
        spanned = spanned_ref[...]
        parity = lax.broadcasted_iota(jnp.int32, spanned.shape, 0) % 2
        mine = parity == place_ref[2]
        total = jnp.zeros_like(spanned)
        for chosen, gram_ref in ((mine, own_ref), (jnp.logical_not(mine), other_ref)):
            a, b, d = gram_ref[:128], gram_ref[128:256], gram_ref[256:]
            squares = jnp.sum(a * a) + 2.0 * jnp.sum(b * b) + jnp.sum(d * d)
            normalizer = 1.7 / jnp.sqrt(jnp.sqrt(squares) + 1e-06)
            oriented = jnp.where(chosen, spanned, 0.0) * normalizer
            gram = jnp.concatenate(
                [jnp.concatenate([a, b], axis=1), jnp.concatenate([b.T, d], axis=1)], axis=0
            )
            total += 1.5 * oriented - 0.5 * jnp.dot(
                oriented,
                gram * (normalizer * normalizer),
                preferred_element_type=f32,
                precision=lax.Precision.HIGHEST,
            )
        out_ref[...] = (math.sqrt(D) * total).astype(bf16).reshape(rows // 2, 2, 256)

    return pl.pallas_call(
        body,
        in_specs=[SMEM] + [VMEM] * 3,
        out_specs=VMEM,
        out_shape=jax.ShapeDtypeStruct((rows // 2, 2, 256), bf16),
        compiler_params=PARAMS,
        cost_estimate=cost(1.8),
    )(place, pin(spanned), pin(own), pin(other))


def update(place, weights, masked, l0, ks, arrays, pieces, earlier):
    rows = weights.shape[0]
    steps = [(l, n) for l in range(len(pieces)) for n in range(len(ks))]

    def where(i, place_ref):
        k = ks[0] + i % len(ks)
        return 0, 0, xor(place_ref[1], k) * 2 + xor(place_ref[2], l0 + i // len(ks))

    def body(place_ref, w_ref, s_ref, *refs):
        held, out_ref, all_ref = refs[: len(arrays)], refs[-2], refs[-1]
        for i, (l, n) in enumerate(steps):

            @pl.when(pl.program_id(0) == i)
            def _():
                for a in range(4):
                    which, at, relative = pieces[l][n][a]
                    group = xor(place_ref[0], a) if relative else a
                    to = pl.ds(pl.multiple_of(group * 128, 128), 128)
                    all_ref[to] = held[which][at]

        change = lax.dot_general(
            s_ref[...], all_ref[...], (((1,), (1,)), ((), ())), preferred_element_type=f32
        )
        at = pl.ds(pl.multiple_of(where(pl.program_id(0), place_ref)[2] * 512, 512), 512)
        out_ref[...] = w_ref[:, :, at] - (change * inv_root).reshape(rows, 2, 512)

    before = [] if earlier is None else [earlier]
    return pl.pallas_call(
        body,
        grid_spec=pltpu.PrefetchScalarGridSpec(
            num_scalar_prefetch=1,
            grid=(len(steps),),
            in_specs=[VMEM] * (2 + len(arrays)) + [pl.BlockSpec(memory_space=pl.ANY)] * len(before),
            out_specs=pl.BlockSpec((rows, 2, 512), where),
            scratch_shapes=[pltpu.VMEM((512, 512), bf16)],
        ),
        out_shape=jax.ShapeDtypeStruct(weights.shape, f32),
        input_output_aliases={3 + len(arrays): 0} if before else {},
        compiler_params=PARAMS,
        cost_estimate=cost(0.5 + len(steps)),
    )(place, weights, pin(masked), *[pin(x) for x in arrays], *before)


def per_device(partials, weights, subspace, moment_one, moment_two):
    rows = weights.shape[0]
    g = lax.axis_index("grp")
    s = lax.axis_index("shard")
    place = jnp.stack([g, s >> 1, s & 1]).astype(jnp.int32)

    def core(x):
        return swap(x, "shard", 1, 8)

    def chip(x, k):
        return swap(x, "shard", 2 * k, 8)

    def group(x, a):
        return swap(x, "grp", a, 4)

    flat = subspace.reshape(2 * rows, 256)
    odd = lax.broadcasted_iota(jnp.int32, flat.shape, 0) % 2 == 1
    zero = jnp.zeros_like(flat)
    masked = jnp.concatenate([jnp.where(odd, zero, flat), jnp.where(odd, flat, zero)], axis=1)

    high = pack(place, partials[0], 1)
    low = pack(after(place, high), partials[0], 0)

    def over_groups(x, y, stay_x, stay_y):
        came_x, came_y = group(x, 1), group(y, 2)
        sum_x, sum_y = pair(stay_x, stay_y, came_x, came_y)
        return [stay_x, came_x, group(sum_x, 2), stay_y, came_y, group(sum_y, 1)]

    high = over_groups(high[0], high[1], after(high[2], low), high[3])
    low = over_groups(*after(low[:2], high[1], high[4]), *low[2:])

    gradient_high, keep, send = project(high, masked)
    chips = chip(add_core(keep, core(send)), 2)
    gradient_low, keep, send = project(low, masked)
    own, following = add_chip(keep, core(after(send, chips)), chips)
    half = finish(own, chip(following, 1))

    gathered = [half] + [group(half, a) for a in (1, 2, 3)]
    late = after(half, gathered[1], gathered[2])
    halves = [half] + [chip(late if k == 1 else half, k) for k in (1, 2, 3)]
    far_half = core(late)
    mine = own_direction(place, half, moment_one, moment_two)

    new_one, new_two, local = moments(place, gathered, moment_one, moment_two)

    halves[3] = after(halves[3], mine)
    halves += [far_half] + [core(h) for h in halves[1:]]
    halves[0] = after(halves[0], gathered[3])
    part = span(gradient_high, gradient_low, halves)
    parts = [part] + [group(part, a) for a in (1, 2, 3)]
    mine = after(mine, part)
    along = [chip(mine, k) for k in (1, 2, 3)]
    spanned, own, other = grams(place, parts)
    own, ship = gram_add(own, core(other))
    own, ship = gram_add(own, chip(ship, 1))
    own, _ = gram_add(own, chip(ship, 2))
    new_subspace = polish(place, spanned, own, core(own))

    along = jnp.stack(along)
    held = [along] + [group(along, a) for a in (1, 2, 3)]
    weights = pin(weights)
    new_weights = update(
        place,
        weights,
        masked,
        0,
        (0,),
        [local, core(local)],
        [[[(l, a, True) for a in range(4)]] for l in range(2)],
        None,
    )
    held = after(held, new_weights, own)
    far = [core(x) for x in held]
    for l, side in ((0, held), (1, far)):
        new_weights = update(
            place,
            weights,
            masked,
            l,
            (1, 2, 3),
            side,
            [[[(a, n, True) for a in range(4)] for n in range(3)]],
            new_weights,
        )
    return new_weights, new_one, new_two, new_subspace


def solution(mesh):
    small = mesh.shape["grp"] == 4 and mesh.shape["shard"] == 8
    return jax.shard_map(
        per_device if small else plain,
        mesh=mesh,
        in_specs=(
            P("grp", "shard", None, None),
            P("shard", None, None),
            P("shard", None, None),
            P("shard", None, None),
            P("shard", None, None),
        ),
        out_specs=(
            P("shard", None, None),
            P("shard", None, None),
            P("shard", None, None),
            P("shard", None, None),
        ),
        check_vma=False,
    )
```

```python
import math

import jax
import jax.numpy as jnp
from jax import lax
from jax.experimental import pallas as pl
from jax.experimental.pallas import tpu as pltpu
from jax.sharding import PartitionSpec as P

D = 1536
bf16 = jnp.bfloat16
f32 = jnp.float32
inv_root = 1.0 / math.sqrt(D)
first_fix = 1.0 - 0.9**10
second_fix = 1.0 - 0.999**10


def plain(partials, weights, subspace, moment_one, moment_two):
    gradient = lax.psum(partials[0], "grp")
    projected = lax.psum_scatter(
        jnp.einsum("dmf,dmk->fmk", gradient, subspace, preferred_element_type=f32) * inv_root,
        "shard",
        scatter_dimension=0,
        tiled=True,
    )
    new_one, new_two, direction = adam(projected, moment_one, moment_two)
    increment = jnp.einsum(
        "dmk,fmk->dmf",
        subspace,
        lax.all_gather(direction, "shard", axis=0, tiled=True),
        preferred_element_type=f32,
    )
    new_weights = weights - increment * inv_root
    spanned = jnp.einsum(
        "dmf,fmk->dmk",
        gradient,
        lax.all_gather(projected.astype(bf16), "shard", axis=0, tiled=True),
        preferred_element_type=f32,
    )
    gram = lax.psum(
        jnp.einsum("dmk,dml->mkl", spanned, spanned, precision=lax.Precision.HIGHEST), "shard"
    )
    normalizer = norm_of(gram, (1, 2))
    oriented = spanned * normalizer[None, :, None]
    ortho_gram = gram * (normalizer * normalizer)[:, None, None]
    polished = 1.5 * oriented - 0.5 * jnp.einsum(
        "dmk,mkl->dml", oriented, ortho_gram, precision=lax.Precision.HIGHEST
    )
    return new_weights, new_one, new_two, (math.sqrt(D) * polished).astype(bf16)


def norm_of(gram, axes):
    return 1.7 / jnp.sqrt(jnp.sqrt(jnp.sum(gram * gram, axis=axes)) + 1e-06)


def adam(projected, one, two):
    new_one = 0.9 * one + 0.1 * projected
    new_two = 0.999 * two + 0.001 * projected * projected
    direction = new_one / first_fix / (jnp.sqrt(new_two / second_fix) + 1e-08)
    return new_one, new_two, direction.astype(bf16)


def swap(x, axis, bit, size):
    return lax.ppermute(x, axis, [(i, i ^ bit) for i in range(size)])


VMEM = pl.BlockSpec(memory_space=pltpu.VMEM)
SMEM = pl.BlockSpec(memory_space=pltpu.SMEM)
PARAMS = pltpu.CompilerParams(vmem_limit_bytes=16 * 2**20)
xor = jnp.bitwise_xor


def pin(x):
    return pltpu.with_memory_space_constraint(x, pltpu.VMEM)


def cost(us):
    return pl.CostEstimate(flops=0, transcendentals=0, bytes_accessed=int(us * 3.5e6))


def call(body, outs, *args, place=None, us=0.3):
    scalars = [] if place is None else [place]
    return pl.pallas_call(
        body,
        in_specs=[SMEM] * len(scalars) + [VMEM] * len(args),
        out_specs=(VMEM,) * len(outs),
        out_shape=tuple(pltpu.VMEM(shape, dtype) for shape, dtype in outs),
        compiler_params=PARAMS,
        cost_estimate=cost(us),
    )(*scalars, *[pin(a) for a in args])


def after(x, *others):
    return lax.optimization_barrier((x, others))[0]


def hbm(x):
    return pltpu.with_memory_space_constraint(x, pltpu.HBM)


def pack(place, x, half):
    rows = x.shape[0]

    def body(place_ref, x_ref, *out_refs):
        i = pl.program_id(0)
        for l, order in ((0, (1, 3, 0, 2)), (1, (2, 3, 0, 1))):

            @pl.when(i // 2 == l)
            def _():
                for n, a in enumerate(order):
                    at = pl.ds(pl.multiple_of(xor(place_ref[0], a) * 128, 128), 128)
                    out_refs[l + n // 2 * 2][n % 2, i % 2] = x_ref[:, :, at].reshape(2 * rows, 128)

    def where(i, place_ref):
        k, l = 2 * half + i % 2, i // 2
        return 0, 0, xor(place_ref[1], k) * 2 + xor(place_ref[2], l)

    return pl.pallas_call(
        body,
        grid_spec=pltpu.PrefetchScalarGridSpec(
            num_scalar_prefetch=1,
            grid=(4,),
            in_specs=[pl.BlockSpec((rows, 2, 512), where)],
            out_specs=(VMEM,) * 4,
        ),
        out_shape=(pltpu.VMEM((2, 2, 2 * rows, 128), bf16),) * 4,
        compiler_params=PARAMS,
        cost_estimate=cost(3.3),
    )(place, hbm(x))


def pair(stay_x, stay_y, came_x, came_y):
    def body(stay_x_ref, stay_y_ref, came_x_ref, came_y_ref, x_ref, y_ref):
        x_ref[...] = (stay_x_ref[1].astype(f32) + came_x_ref[1].astype(f32)).astype(bf16)
        y_ref[...] = (stay_y_ref[1].astype(f32) + came_y_ref[1].astype(f32)).astype(bf16)

    out = (stay_x.shape[1:], bf16)
    return call(body, [out, out], stay_x, stay_y, came_x, came_y)


def project(held, masked):
    rows = masked.shape[0]

    def body(*refs):
        sides, (s_ref, g_ref, keep_ref, send_ref) = (refs[:3], refs[3:6]), refs[6:]
        for i in (2, 3, 0, 1):
            stay, came, last = sides[i // 2]
            total = (stay[0, i % 2].astype(f32) + came[0, i % 2].astype(f32)) + last[i % 2].astype(
                f32
            )
            gradient = total.astype(bf16)
            g_ref[i] = gradient
            part = lax.dot_general(
                gradient, s_ref[...], (((0,), (0,)), ((), ())), preferred_element_type=f32
            )
            if i < 2:
                keep_ref[i] = part
            else:
                send_ref[i - 2] = part.astype(bf16)

    return call(
        body,
        [((4, rows, 128), bf16), ((2, 128, 512), f32), ((2, 128, 512), bf16)],
        *held,
        masked,
        us=0.01,
    )


def add_core(keep, came):
    def body(keep_ref, came_ref, out_ref):
        out_ref[...] = (keep_ref[...] + came_ref[...].astype(f32)).astype(bf16)

    return call(body, [((2, 128, 512), bf16)], keep, came)[0]


def add_chip(keep, came, chips):
    def body(keep_ref, came_ref, chips_ref, own_ref, next_ref):
        total = keep_ref[...] + came_ref[...].astype(f32) + chips_ref[...].astype(f32)
        own_ref[...] = total[0]
        next_ref[...] = total[1].astype(bf16)

    return call(body, [((128, 512), f32), ((128, 512), bf16)], keep, came, chips)


def finish(own, came):
    def body(own_ref, came_ref, half_ref):
        half_ref[...] = ((own_ref[...] + came_ref[...].astype(f32)) * inv_root).astype(bf16)

    return call(body, [((128, 512), bf16)], own, came)[0]


def own_direction(place, half, one, two):
    def body(place_ref, half_ref, one_ref, two_ref, own_ref):
        at = pl.ds(pl.multiple_of(place_ref[0] * 128, 128), 128)
        for m in range(2):
            lanes = slice(256 * m, 256 * (m + 1))
            projected = half_ref[:, lanes].astype(f32)
            own_ref[:, lanes] = adam(projected, one_ref[at, m, :], two_ref[at, m, :])[2]

    return call(body, [((128, 512), bf16)], half, one, two, place=place, us=0.9)[0]


def moments(place, gathered, one, two):
    def body(place_ref, *refs):
        halves, (one_ref, two_ref, new_one_ref, new_two_ref, all_ref) = refs[:4], refs[4:]
        for a in range(4):
            at = pl.ds(pl.multiple_of(xor(place_ref[0], a) * 128, 128), 128)
            for m in range(2):
                lanes = slice(256 * m, 256 * (m + 1))
                projected = halves[a][:, lanes].astype(f32)
                new_one, new_two, direction = adam(projected, one_ref[at, m, :], two_ref[at, m, :])
                new_one_ref[at, m, :] = new_one
                new_two_ref[at, m, :] = new_two
                all_ref[a, :, lanes] = direction

    return pl.pallas_call(
        body,
        in_specs=[SMEM] + [VMEM] * 6,
        out_specs=(VMEM,) * 3,
        out_shape=(
            jax.ShapeDtypeStruct(one.shape, f32),
            jax.ShapeDtypeStruct(one.shape, f32),
            pltpu.VMEM((4, 128, 512), bf16),
        ),
        compiler_params=PARAMS,
        cost_estimate=cost(3.5),
    )(place, *[pin(x) for x in gathered], one, two)


def span(high, low, pieces):
    rows = high.shape[1]

    def body(high_ref, low_ref, *refs):
        p_refs, out_ref = refs[:8], refs[8]
        total = None
        for l in range(2):
            for k in range(4):
                g_ref = high_ref if k >= 2 else low_ref
                term = jnp.dot(
                    g_ref[l * 2 + k % 2], p_refs[l * 4 + k][...], preferred_element_type=f32
                )
                total = term if total is None else total + term
        odd = lax.broadcasted_iota(jnp.int32, (rows, 256), 0) % 2 == 1
        out_ref[...] = jnp.where(odd, total[:, 256:], total[:, :256]).astype(bf16)

    return call(body, [((rows, 256), bf16)], high, low, *pieces, us=1.0)[0]


def grams(place, parts):
    rows = parts[0].shape[0]

    def body(place_ref, a_ref, b_ref, c_ref, d_ref, spanned_ref, own_ref, other_ref):
        spanned = (a_ref[...].astype(f32) + b_ref[...].astype(f32)) + (
            c_ref[...].astype(f32) + d_ref[...].astype(f32)
        )
        spanned_ref[...] = spanned
        parity = lax.broadcasted_iota(jnp.int32, spanned.shape, 0) % 2
        mine = jnp.where(parity == place_ref[2], spanned, 0.0)
        theirs = jnp.where(parity == place_ref[2], 0.0, spanned)
        for part, out_ref in ((theirs, other_ref), (mine, own_ref)):
            left, right = part[:, :128], part[:, 128:]
            for i, (x, y) in enumerate(((left, left), (left, right), (right, right))):
                out_ref[128 * i : 128 * (i + 1)] = lax.dot_general(
                    x,
                    y,
                    (((0,), (0,)), ((), ())),
                    preferred_element_type=f32,
                    precision=lax.Precision.HIGHEST,
                )

    blocks = ((384, 128), f32)
    return call(body, [((rows, 256), f32), blocks, blocks], *parts, place=place, us=1.8)


def gram_add(own, came):
    def body(own_ref, came_ref, sum_ref, ship_ref):
        total = own_ref[...] + came_ref[...].astype(f32)
        sum_ref[...] = total
        ship_ref[...] = total.astype(bf16)

    return call(body, [((384, 128), f32), ((384, 128), bf16)], own, came)


def polish(place, spanned, own, other):
    rows = spanned.shape[0]

    def body(place_ref, spanned_ref, own_ref, other_ref, out_ref):
        spanned = spanned_ref[...]
        parity = lax.broadcasted_iota(jnp.int32, spanned.shape, 0) % 2
        mine = parity == place_ref[2]
        total = jnp.zeros_like(spanned)
        for chosen, gram_ref in ((mine, own_ref), (jnp.logical_not(mine), other_ref)):
            a, b, d = gram_ref[:128], gram_ref[128:256], gram_ref[256:]
            squares = jnp.sum(a * a) + 2.0 * jnp.sum(b * b) + jnp.sum(d * d)
            normalizer = 1.7 / jnp.sqrt(jnp.sqrt(squares) + 1e-06)
            oriented = jnp.where(chosen, spanned, 0.0) * normalizer
            gram = jnp.concatenate(
                [jnp.concatenate([a, b], axis=1), jnp.concatenate([b.T, d], axis=1)], axis=0
            )
            total += 1.5 * oriented - 0.5 * jnp.dot(
                oriented,
                gram * (normalizer * normalizer),
                preferred_element_type=f32,
                precision=lax.Precision.HIGHEST,
            )
        out_ref[...] = (math.sqrt(D) * total).astype(bf16).reshape(rows // 2, 2, 256)

    return pl.pallas_call(
        body,
        in_specs=[SMEM] + [VMEM] * 3,
        out_specs=VMEM,
        out_shape=jax.ShapeDtypeStruct((rows // 2, 2, 256), bf16),
        compiler_params=PARAMS,
        cost_estimate=cost(1.8),
    )(place, pin(spanned), pin(own), pin(other))


def update(place, weights, masked, l0, ks, arrays, pieces, earlier):
    rows = weights.shape[0]
    steps = [(l, n) for l in range(len(pieces)) for n in range(len(ks))]

    def where(i, place_ref):
        k = ks[0] + i % len(ks)
        return 0, 0, xor(place_ref[1], k) * 2 + xor(place_ref[2], l0 + i // len(ks))

    def body(place_ref, w_ref, s_ref, *refs):
        held, out_ref, all_ref = refs[: len(arrays)], refs[-2], refs[-1]
        for i, (l, n) in enumerate(steps):

            @pl.when(pl.program_id(0) == i)
            def _():
                for a in range(4):
                    which, at, relative = pieces[l][n][a]
                    group = xor(place_ref[0], a) if relative else a
                    to = pl.ds(pl.multiple_of(group * 128, 128), 128)
                    all_ref[to] = held[which][at]

        change = lax.dot_general(
            s_ref[...], all_ref[...], (((1,), (1,)), ((), ())), preferred_element_type=f32
        )
        at = pl.ds(pl.multiple_of(where(pl.program_id(0), place_ref)[2] * 512, 512), 512)
        out_ref[...] = w_ref[:, :, at] - (change * inv_root).reshape(rows, 2, 512)

    before = [] if earlier is None else [earlier]
    return pl.pallas_call(
        body,
        grid_spec=pltpu.PrefetchScalarGridSpec(
            num_scalar_prefetch=1,
            grid=(len(steps),),
            in_specs=[VMEM] * (2 + len(arrays)) + [pl.BlockSpec(memory_space=pl.ANY)] * len(before),
            out_specs=pl.BlockSpec((rows, 2, 512), where),
            scratch_shapes=[pltpu.VMEM((512, 512), bf16)],
        ),
        out_shape=jax.ShapeDtypeStruct(weights.shape, f32),
        input_output_aliases={3 + len(arrays): 0} if before else {},
        compiler_params=PARAMS,
        cost_estimate=cost(0.5 + len(steps)),
    )(place, weights, pin(masked), *[pin(x) for x in arrays], *before)


def per_device(partials, weights, subspace, moment_one, moment_two):
    rows = weights.shape[0]
    g = lax.axis_index("grp")
    s = lax.axis_index("shard")
    place = jnp.stack([g, s >> 1, s & 1]).astype(jnp.int32)

    def core(x):
        return swap(x, "shard", 1, 8)

    def chip(x, k):
        return swap(x, "shard", 2 * k, 8)

    def group(x, a):
        return swap(x, "grp", a, 4)

    flat = subspace.reshape(2 * rows, 256)
    odd = lax.broadcasted_iota(jnp.int32, flat.shape, 0) % 2 == 1
    zero = jnp.zeros_like(flat)
    masked = jnp.concatenate([jnp.where(odd, zero, flat), jnp.where(odd, flat, zero)], axis=1)

    high = pack(place, partials[0], 1)
    low = pack(after(place, high), partials[0], 0)

    def over_groups(x, y, stay_x, stay_y):
        came_x, came_y = group(x, 1), group(y, 2)
        sum_x, sum_y = pair(stay_x, stay_y, came_x, came_y)
        return [stay_x, came_x, group(sum_x, 2), stay_y, came_y, group(sum_y, 1)]

    high = over_groups(high[0], high[1], after(high[2], low), high[3])
    low = over_groups(*after(low[:2], high[1], high[4]), *low[2:])

    gradient_high, keep, send = project(high, masked)
    chips = chip(add_core(keep, core(send)), 2)
    gradient_low, keep, send = project(low, masked)
    own, following = add_chip(keep, core(after(send, chips)), chips)
    half = finish(own, chip(following, 1))

    gathered = [half] + [group(half, a) for a in (1, 2, 3)]
    late = after(half, gathered[1])
    halves = [half] + [chip(late if k == 1 else half, k) for k in (1, 2, 3)]
    far_half = core(late)
    mine = own_direction(place, half, moment_one, moment_two)

    new_one, new_two, local = moments(place, gathered, moment_one, moment_two)

    halves[3] = after(halves[3], mine)
    halves += [far_half] + [core(h) for h in halves[1:]]
    halves[0] = after(halves[0], gathered[2], gathered[3])
    part = span(gradient_high, gradient_low, halves)
    parts = [part] + [group(part, a) for a in (1, 2, 3)]
    mine = after(mine, part)
    along = [chip(mine, k) for k in (1, 2, 3)]
    spanned, own, other = grams(place, parts)
    own, ship = gram_add(own, core(other))
    own, ship = gram_add(own, chip(ship, 1))
    own, _ = gram_add(own, chip(ship, 2))
    new_subspace = polish(place, spanned, own, core(own))

    along = jnp.stack(along)
    held = [along] + [group(along, a) for a in (1, 2, 3)]
    weights = pin(weights)
    new_weights = update(
        place,
        weights,
        masked,
        0,
        (0,),
        [local, core(local)],
        [[[(l, a, True) for a in range(4)]] for l in range(2)],
        None,
    )
    held = after(held, new_weights, own)
    far = [core(x) for x in held]
    for l, side in ((0, held), (1, far)):
        new_weights = update(
            place,
            weights,
            masked,
            l,
            (1, 2, 3),
            side,
            [[[(a, n, True) for a in range(4)] for n in range(3)]],
            new_weights,
        )
    return new_weights, new_one, new_two, new_subspace


def solution(mesh):
    small = mesh.shape["grp"] == 4 and mesh.shape["shard"] == 8
    return jax.shard_map(
        per_device if small else plain,
        mesh=mesh,
        in_specs=(
            P("grp", "shard", None, None),
            P("shard", None, None),
            P("shard", None, None),
            P("shard", None, None),
            P("shard", None, None),
        ),
        out_specs=(
            P("shard", None, None),
            P("shard", None, None),
            P("shard", None, None),
            P("shard", None, None),
        ),
        check_vma=False,
    )
```
